32 devices in a mesh: blk: 8 (over z, x), grid: 4 (over y, core).
Axes of the slice: x: 2, y: 2, z: 4, core: 2. Of those that a mesh axis runs over, the one named last changes fastest.
Arguments:
- patches: bfloat16 [4, 1024, 1024], P('grid', 'blk'), may hold values from -6 to 6
- stem_weight: bfloat16 [2, 1024, 768], replicated, may hold values from -0.125 to 0.125
- norm_gain: bfloat16 [768], replicated, may hold values from 0.25 to 1.75
- w_qkv: bfloat16 [768, 1280], replicated, may hold values from -0.21875 to 0.21875
- w_out: bfloat16 [768, 768], replicated, may hold values from -0.21875 to 0.21875
- per_head_scale: float32 [12], replicated, may hold values from 0.05 to 1, as said below
- positions: int32 [1024], replicated, may hold values from 0 to 1023, each once
- d_out: bfloat16 [4, 1024, 768], P('grid', 'blk'), may hold values from -48 to 48
Outputs:
- d_stem_weight: float32 [2, 1024, 768], P(None, None, ('blk', 'grid'))
- d_norm_gain: float32 [768], P(('blk', 'grid'))
- d_w_qkv: float32 [768, 1280], P(('blk', 'grid'))
- d_w_out: float32 [768, 768], P(None, ('blk', 'grid'))
The draws below stay inside these ranges and needn't reach their ends.
Inputs may be any that keep to these rules, and one draw needn't show every extreme that they name: A permutation of the 1024 positions of a band. `per_head_scale`: positive.
All inputs are finite; a program needn't handle non-finite values.
Results may differ from the reference program's by a relative error of at most 0.015.
The reference program's roundings to bfloat16 on the way count: a program that leaves them out, or rounds other values in their place, can miss the bound.
Values may be sent and summed in bfloat16 or wider, within the bound.
A program may use at most 128 MiB of HBM per device.

```python
from functools import partial
import jax
import jax.numpy as jnp
from jax import lax

D = 768
QUERY_HEADS = 12
KEY_VALUE_HEADS = 4
HEAD_SIZE = 64
TR = 8
TC = 16
TOK_DEV = 128
BAND_TOKENS = 1024
PIN = 1024
QD = 768
KD = 256
N_BLK = 8
N_GRID = 4


def draw_per_head_scale(key, part):
    lowest, highest = (0.05, 0.4)
    uniform_draw = jax.random.uniform(key, (QUERY_HEADS,), jnp.float32)
    return jnp.exp(jnp.log(lowest) + uniform_draw * (jnp.log(highest) - jnp.log(lowest)))


def draw_d_out(key, part):
    noise_key = jax.random.fold_in(key, 11)
    order_key = jax.random.fold_in(key, 23)
    owners = N_BLK * N_GRID
    noise = jnp.clip(jax.random.normal(noise_key, (N_GRID, BAND_TOKENS, D), jnp.float32), -6.0, 6.0)
    factor = 8.0
    pairing = jax.random.permutation(order_key, owners).astype(jnp.int32)
    band_index = jnp.arange(N_GRID, dtype=jnp.int32)[:, None]
    block_index = (jnp.arange(BAND_TOKENS, dtype=jnp.int32) // TOK_DEV)[None, :]
    owner = block_index * N_GRID + band_index
    target = jnp.take(pairing, owner.reshape(-1)).reshape(N_GRID, BAND_TOKENS, 1)
    column_block = (jnp.arange(D, dtype=jnp.int32) // (D // owners))[None, None, :]
    heavy = jnp.where(target == column_block, factor, 1.0)
    return jnp.clip(noise * heavy, -48.0, 48.0).astype(jnp.bfloat16)


def block_scale(key, extent, cuts, least, high):
    factor_of, own = 1.0, jax.random.fold_in(key, 6)
    for position, blocks in cuts:
        draws = jnp.exp(jax.random.uniform(jax.random.fold_in(own, position), (blocks,), jnp.float32, least / len(cuts), high / len(cuts)))
        factor_of = factor_of * jnp.repeat(draws, extent[position] // blocks).reshape([-1 if axis == position else 1 for axis in range(len(extent))])
    return factor_of


def scatter_about(own_key, extent, deviation, most, cuts=(), kind=jnp.bfloat16):
    result = jax.random.normal(own_key, extent, jnp.float32) * deviation
    if len(cuts) > 0:
        result = block_scale(own_key, extent, cuts, -0.22, 0.18) * result
    return jnp.clip(result, min=-most, max=most).astype(kind)


def setup_inputs(seed: int = 0) -> dict:
    seeds = jax.random.split(jax.random.key(seed), 9)
    patches = scatter_about(seeds[0], (N_GRID, BAND_TOKENS, PIN), 1.0, 6.0, ((0, 4), (1, 8)))
    stem_weight = scatter_about(seeds[1], (2, PIN, D), (2 * PIN) ** -0.5, 0.125)
    norm_gain = jnp.clip(1.0 + 0.15 * jax.random.normal(seeds[2], (D,), jnp.float32), 0.25, 1.75).astype(jnp.bfloat16)
    w_qkv = scatter_about(seeds[3], (D, QD + 2 * KD), D ** -0.5, 0.21875)
    w_out = scatter_about(seeds[4], (QD, D), QD ** -0.5, 0.21875)
    per_head_scale = draw_per_head_scale(jax.random.fold_in(seeds[8], 71), 0)
    positions = jax.random.permutation(seeds[6], BAND_TOKENS).astype(jnp.int32)
    d_out = draw_d_out(jax.random.fold_in(seeds[8], 71), 0)
    return dict(patches=patches, stem_weight=stem_weight, norm_gain=norm_gain, w_qkv=w_qkv, w_out=w_out, per_head_scale=per_head_scale, positions=positions, d_out=d_out)


def lower(values):
    return lax.optimization_barrier(values.astype(jnp.bfloat16))

def row_norm(values):
    return values * lax.rsqrt(lax.optimization_barrier(jnp.mean(values * values, axis=-1, keepdims=True)) + 1e-05)

def head_norm(values):
    return values * lax.rsqrt(lax.optimization_barrier(jnp.mean(values * values, axis=-1, keepdims=True)) + 1e-06)

def window_blocks(array):
    blocks = array.reshape((N_BLK, TOK_DEV) + array.shape[1:])
    return jnp.concatenate([jnp.roll(blocks, offset, axis=0) for offset in range(4)], axis=1)

def attend_block(per_head_scale, inputs):
    query_tile_block, gradient_block, key_band_window, value_band_window, query_pos, key_pos = inputs
    group_factor = QUERY_HEADS // KEY_VALUE_HEADS
    token_row_count = query_tile_block.shape[0]
    every_key = key_band_window.shape[0]
    visible = (key_pos[None, :] <= query_pos[:, None])[None, None]
    query_wide = query_tile_block.astype(jnp.float32).reshape(token_row_count, KEY_VALUE_HEADS, group_factor, HEAD_SIZE)
    gradient_wide = gradient_block.astype(jnp.float32).reshape(token_row_count, KEY_VALUE_HEADS, group_factor, HEAD_SIZE)
    key_wide = key_band_window.astype(jnp.float32).reshape(every_key, KEY_VALUE_HEADS, HEAD_SIZE)
    value_wide = value_band_window.astype(jnp.float32).reshape(every_key, KEY_VALUE_HEADS, HEAD_SIZE)
    score_scale = per_head_scale.astype(jnp.float32).reshape(KEY_VALUE_HEADS, group_factor)[:, :, None, None]
    attention_scores = jnp.einsum('phiv,chv->hipc', query_wide, key_wide) * score_scale
    attention_scores = jnp.where(visible, attention_scores, -1e+30)
    top = lax.optimization_barrier(jnp.max(attention_scores, axis=-1, keepdims=True))
    weights = jnp.where(visible, jnp.exp(attention_scores - top), 0.0)
    probs = weights / lax.optimization_barrier(jnp.sum(weights, axis=-1, keepdims=True))
    probability_narrow = lower(probs).astype(jnp.float32)
    attention_output = jnp.einsum('ychp,pyu->hycu', probability_narrow, value_wide)
    softmax_delta = jnp.einsum('pyui,pyui->yup', gradient_wide, attention_output)
    probability_gradient = jnp.einsum('phiv,chv->hipc', gradient_wide, value_wide)
    score_gradient = lower(score_scale * probs * (probability_gradient - softmax_delta[..., None])).astype(jnp.float32)
    query_gradient = jnp.einsum('ychp,pyu->hycu', score_gradient, key_wide).reshape(token_row_count, QUERY_HEADS * HEAD_SIZE)
    key_gradient = jnp.einsum('lpma,mlpx->alx', score_gradient, query_wide).reshape(every_key, KEY_VALUE_HEADS * HEAD_SIZE)
    value_gradient = jnp.einsum('lpma,mlpx->alx', probability_narrow, gradient_wide).reshape(every_key, KEY_VALUE_HEADS * HEAD_SIZE)
    return (attention_output.reshape(token_row_count, QUERY_HEADS * HEAD_SIZE), query_gradient, jnp.concatenate([key_gradient, value_gradient], axis=1))

def band_terms(patches, below, stem_weight, norm_gain, w_qkv, w_out, per_head_scale, positions, d_out):
    query_span_width = QUERY_HEADS * HEAD_SIZE
    key_span_width = KEY_VALUE_HEADS * HEAD_SIZE
    stem = jnp.dot(patches, stem_weight[0], preferred_element_type=jnp.float32)
    stem = stem + jnp.dot(below, stem_weight[1], preferred_element_type=jnp.float32)
    token_f = lower(stem).astype(jnp.float32)
    gain_f = norm_gain.astype(jnp.float32)
    normed = row_norm(token_f)
    hidden = lower(normed * gain_f)
    query_key_value = jnp.dot(hidden, w_qkv, preferred_element_type=jnp.float32)
    query = query_key_value[:, :query_span_width].reshape(BAND_TOKENS, QUERY_HEADS, HEAD_SIZE)
    key = query_key_value[:, query_span_width:query_span_width + key_span_width].reshape(BAND_TOKENS, KEY_VALUE_HEADS, HEAD_SIZE)
    query_normalized = lower(head_norm(query)).reshape(BAND_TOKENS, query_span_width)
    key_n = lower(head_norm(key)).reshape(BAND_TOKENS, key_span_width)
    value = lower(query_key_value[:, query_span_width + key_span_width:])
    attention_gradient = lower(jnp.dot(d_out, w_out.T, preferred_element_type=jnp.float32))
    attn_f, query_gradient, dkv = lax.map(partial(attend_block, per_head_scale), (query_normalized.reshape(N_BLK, TOK_DEV, query_span_width), attention_gradient.reshape(N_BLK, TOK_DEV, query_span_width), window_blocks(key_n), window_blocks(value), positions.reshape(N_BLK, TOK_DEV), window_blocks(positions)))
    attention_output = lower(attn_f.reshape(BAND_TOKENS, query_span_width))
    key_value_gradient_sum = jnp.zeros((N_BLK, TOK_DEV, 2 * key_span_width), jnp.float32)
    for offset in range(4):
        key_value_gradient_sum = key_value_gradient_sum + jnp.roll(dkv[:, offset * TOK_DEV:(offset + 1) * TOK_DEV], -offset, axis=0)
    key_value_gradient_sum = key_value_gradient_sum.reshape(BAND_TOKENS, 2 * key_span_width)
    pull_query = jax.vjp(head_norm, query)[1]
    gather_key = jax.vjp(head_norm, key)[1]
    dq_full = pull_query(query_gradient.reshape(BAND_TOKENS, QUERY_HEADS, HEAD_SIZE))[0].reshape(BAND_TOKENS, query_span_width)
    key_gradient_whole = gather_key(key_value_gradient_sum[:, :key_span_width].reshape(BAND_TOKENS, KEY_VALUE_HEADS, HEAD_SIZE))[0].reshape(BAND_TOKENS, key_span_width)
    d_qkv = lower(jnp.concatenate([dq_full, key_gradient_whole, key_value_gradient_sum[:, key_span_width:]], axis=1))
    d_w_qkv = jnp.dot(hidden.T, d_qkv, preferred_element_type=jnp.float32)
    d_w_out = jnp.dot(attention_output.T, d_out, preferred_element_type=jnp.float32)
    d_hidden = jnp.dot(d_qkv, w_qkv.T, preferred_element_type=jnp.float32)
    d_gain = lax.optimization_barrier(jnp.sum(d_hidden * normed, axis=0))
    pull_tokens = jax.vjp(row_norm, token_f)[1]
    d_tokens = lower(d_out.astype(jnp.float32) + pull_tokens(d_hidden * gain_f)[0])
    d_stem = jnp.stack([jnp.dot(patches.T, d_tokens, preferred_element_type=jnp.float32), jnp.dot(below.T, d_tokens, preferred_element_type=jnp.float32)])
    return (d_stem, d_gain, d_w_qkv, d_w_out)

def reference(patches, stem_weight, norm_gain, w_qkv, w_out, per_head_scale, positions, d_out):
    image = patches.reshape(N_GRID, N_BLK, TR, TC, PIN).transpose(0, 2, 1, 3, 4).reshape(N_GRID * TR, N_BLK, TC, PIN)
    shifted = jnp.concatenate([image[1:], jnp.zeros_like(image[:1])], axis=0)
    below = shifted.reshape(N_GRID, TR, N_BLK, TC, PIN).transpose(0, 2, 1, 3, 4).reshape(N_GRID, BAND_TOKENS, PIN)
    totals = band_terms(patches[0], below[0], stem_weight, norm_gain, w_qkv, w_out, per_head_scale, positions, d_out[0])
    for band in range(1, N_GRID):
        terms = band_terms(patches[band], below[band], stem_weight, norm_gain, w_qkv, w_out, per_head_scale, positions, d_out[band])
        totals = jax.tree.map(lambda first, second: first + second, totals, terms)
    return (totals[0], totals[1], totals[2], totals[3])
```

```python
from functools import partial

import jax
import jax.numpy as jnp
from jax import lax
from jax.experimental import pallas as pl
from jax.experimental.pallas import tpu as pltpu
from jax.sharding import PartitionSpec as P

QUERY_HEADS = 12
KEY_VALUE_HEADS = 4
HEAD_SIZE = 64
TC = 16


def shifted(x, axis, by):
    peers = lax.axis_size(axis)
    pairs = [(i, i + by) for i in range(peers) if 0 <= i + by < peers]
    return lax.ppermute(x, axis, pairs)


def passed_along(x, axis, by):
    peers = lax.axis_size(axis)
    return lax.ppermute(x, axis, [(i, (i + by) % peers) for i in range(peers)])


def row_norm(values):
    return values * lax.rsqrt(jnp.mean(values * values, axis=-1, keepdims=True) + 1e-05)


def head_norm(values):
    return values * lax.rsqrt(jnp.mean(values * values, axis=-1, keepdims=True) + 1e-06)


def transposed_dot(a, b):
    return lax.dot_general(a, b, (((0,), (0,)), ((), ())), preferred_element_type=jnp.float32)


def rowwise_dot(a, b):
    return lax.dot_general(a, b, (((1,), (1,)), ((), ())), preferred_element_type=jnp.float32)


def plain_dot(a, b):
    return jnp.dot(a, b, preferred_element_type=jnp.float32)


def half_sums(x):
    low = lax.broadcasted_iota(jnp.int32, x.shape, 1) < HEAD_SIZE
    first = jnp.sum(jnp.where(low, x, 0.0), axis=1, keepdims=True)
    second = jnp.sum(jnp.where(low, 0.0, x), axis=1, keepdims=True)
    return jnp.where(low, first, second)


def fits_planes(width):
    blocks, bands = lax.axis_size("blk"), lax.axis_size("grid")
    devices = blocks * bands
    return bands == 4 and blocks % 2 == 0 and blocks >= 4 and width % devices == 0 and (width // devices) % 8 == 0


def layer_kernel(plan, *refs):
    nz, parts = plan
    (scale_ref, tiles_hbm, grad_hbm, stem_hbm, gain_ref, wqkv_hbm, wout_hbm, pos_ref) = refs[:8]
    (stem_out, gain_out, qkv_out, out_out) = refs[8:12]
    scratch = list(refs[12:])
    count = len(parts)
    first = [scratch.pop(0) for _ in range(count)]
    got_a = [scratch.pop(0) for _ in range(count)]
    send_b = [scratch.pop(0) for _ in range(count)]
    got_b = [scratch.pop(0) for _ in range(count)]
    send_z = [scratch.pop(0) for _ in range(count)]
    got_z = [scratch.pop(0) for _ in range(count)]
    (final, final_recv, stem_w, wqkv, wout, image, halo_rows, grad_pair, hidden_pair, attn_pair, dq_pair, dkv_pair,
     kv, dkv_out, dkv_own, dkv_in, normed_ref, inv_ref, qk_ref, heads_inv, qn, da, attn, dq, dqkv,
     tok_out, tok_all, stem_send, stem_got, gain_own, gain_got, gain_plane, gain_z, gain_col,
     load_sem, pair_send, pair_got, final_send, final_got, halo_send, halo_got, tile_send, tile_got, pass_send, pass_got,
     kv_send, kv_got, dkv_send, dkv_got, part_send, part_got, z_send, z_got, tok_send, tok_got, gain_send, gain_arrived,
     gain_z_send, gain_z_got, stem_sent, stem_arrived) = scratch
    tok, width = grad_pair.shape[1:]
    halo = halo_rows.shape[0]
    pin = image.shape[2]
    span = kv.shape[0] * 128
    group = QUERY_HEADS // KEY_VALUE_HEADS
    own_blk = lax.axis_index("blk")
    own_grid = lax.axis_index("grid")
    blk_count = lax.axis_size("blk")
    grid_count = lax.axis_size("grid")
    core = own_grid % 2
    own_y = own_grid // 2
    own_x = own_blk % 2
    own_z = own_blk // 2
    rows = width // (blk_count * grid_count)
    other_core = {"blk": own_blk, "grid": own_grid + 1 - 2 * core}
    above = {"blk": own_blk, "grid": (own_grid + grid_count - 1) % grid_count}
    plane = [(i, j) for i in range(2) for j in range(grid_count) if i + j > 0]

    def along(offset):
        return {"blk": (own_blk + offset + blk_count) % blk_count, "grid": own_grid}

    def beside(i, j):
        return {"blk": own_z * 2 + (own_x + i) % 2, "grid": (own_grid + j) % grid_count}

    def level(k):
        return {"blk": (own_z + k) % nz * 2 + own_x, "grid": own_grid}

    own_rows = pl.ds(pl.multiple_of(own_grid * tok, tok), tok)
    loads = [
        pltpu.make_async_copy(tiles_hbm, image.at[own_x, own_rows], load_sem.at[0]),
        pltpu.make_async_copy(stem_hbm.at[0], stem_w.at[0], load_sem.at[1]),
        pltpu.make_async_copy(stem_hbm.at[1], stem_w.at[1], load_sem.at[2]),
        pltpu.make_async_copy(wqkv_hbm, wqkv, load_sem.at[3]),
        pltpu.make_async_copy(grad_hbm, grad_pair.at[core], load_sem.at[4]),
        pltpu.make_async_copy(wout_hbm, wout, load_sem.at[5]),
    ]
    barrier = pltpu.get_barrier_semaphore()
    peers = [beside(i, j) for i, j in plane] + [level(k) for k in range(1, nz)] + [along(j) for j in (1, 2, 3, -1, -2, -3)]
    for peer in peers:
        pl.semaphore_signal(barrier, inc=1, device_id=peer, device_id_type=pl.DeviceIdType.MESH)
    for load in loads:
        load.start()
    image[:, grid_count * tok :] = jnp.zeros((2, halo, pin), image.dtype)

    def push(source, target, sems, got, device):
        copy = pltpu.make_async_remote_copy(
            src_ref=source, dst_ref=target, send_sem=sems, recv_sem=got, device_id=device, device_id_type=pl.DeviceIdType.MESH
        )
        copy.start()
        return copy

    def pair(which, source, target):
        return push(source, target, pair_send.at[which], pair_got.at[which], other_core)

    def tiles_to(slot, i, j):
        mine = image.at[own_x, own_rows]
        return push(mine, mine, tile_send.at[slot], tile_got.at[slot], beside(i, j))

    loads[0].wait()
    pl.semaphore_wait(barrier, len(peers))
    halo_copy = push(image.at[own_x, pl.ds(pl.multiple_of(own_grid * tok, tok), halo)], halo_rows, halo_send, halo_got, above)
    tile_copies = [tiles_to(0, 0, 2)]
    tile_pair = pair(0, image.at[own_x, own_rows], image.at[own_x, own_rows])

    loads[1].wait()
    tiles = image[own_x, own_rows]
    stem = plain_dot(tiles, stem_w[0])
    loads[2].wait()
    halo_copy.wait()

    @pl.when(own_grid == grid_count - 1)
    def _():
        halo_rows[...] = jnp.zeros(halo_rows.shape, halo_rows.dtype)

    below = jnp.concatenate([tiles[halo:], halo_rows[...]], axis=0)
    stem = stem + plain_dot(below, stem_w[1])
    token_f = stem.astype(jnp.bfloat16).astype(jnp.float32)
    inv = lax.rsqrt(jnp.sum(token_f * token_f, axis=1, keepdims=True) / width + 1e-05)
    normed = token_f * inv
    normed_ref[...] = normed
    inv_ref[...] = jnp.broadcast_to(inv, inv_ref.shape)
    gain_f = gain_ref[...].astype(jnp.float32).reshape(1, width)
    hidden = (normed * gain_f).astype(jnp.bfloat16)
    hidden_pair[core] = hidden
    loads[3].wait()
    key_start = QUERY_HEADS * HEAD_SIZE

    def normalize(x):
        scale = lax.rsqrt(half_sums(x * x) / HEAD_SIZE + 1e-06)
        return scale, (x * scale).astype(jnp.bfloat16)

    keys = plain_dot(hidden, wqkv[:, key_start:])
    kv_copies = []
    for u in range(span // 128):
        at = u * 128
        heads_inv[:, key_start + at : key_start + at + 128], kv[u, 0, :, :128] = normalize(keys[:, at : at + 128])
        kv[u, 0, :, 128:] = keys[:, span + at : span + at + 128].astype(jnp.bfloat16)
        kv_copies.append([push(kv.at[u, 0], kv.at[u, j], kv_send.at[u, j], kv_got.at[u, j], along(j)) for j in (3, 2, 1)])
    qk_ref[:, key_start:] = keys[:, :span]
    tile_copies.append(tiles_to(1, 1, 0))
    tile_copies.append(tiles_to(2, 1, 2))
    loads[4].wait()
    grad_copy = pair(1, grad_pair.at[core], grad_pair.at[core])
    hidden_copy = pair(2, hidden_pair.at[core], hidden_pair.at[core])
    queries = plain_dot(hidden, wqkv[:, :key_start])
    qk_ref[:, :key_start] = queries
    for at in range(0, key_start, 128):
        heads_inv[:, at : at + 128], qn[:, at : at + 128] = normalize(queries[:, at : at + 128])
    loads[5].wait()
    grad_own = grad_pair[core]
    da[...] = rowwise_dot(grad_own, wout[...]).astype(jnp.bfloat16)

    query_pos = pos_ref[pl.ds(own_blk, 1), :]
    seen = []
    for j in range(4):
        key_pos = pos_ref[pl.ds((own_blk + blk_count - j) % blk_count, 1), :]
        column = jnp.broadcast_to(key_pos, (tok, tok)).T
        seen.append(column <= query_pos)
    visible = jnp.concatenate([jnp.where(x, 1.0, 0.0) for x in seen], axis=0) > 0.5
    dkv_copies = []
    for g in range(KEY_VALUE_HEADS):
        u, low_lane = g // 2, g % 2 * HEAD_SIZE
        lanes = slice(low_lane, low_lane + HEAD_SIZE)
        value_lanes = slice(128 + low_lane, 128 + low_lane + HEAD_SIZE)
        if g % 2 == 0:
            for copy in kv_copies[u]:
                copy.wait()
        keys_g = kv[u, :, :, lanes].reshape(4 * tok, HEAD_SIZE)
        values_g = kv[u, :, :, value_lanes].reshape(4 * tok, HEAD_SIZE)
        heads = [slice((g * group + i) * HEAD_SIZE, (g * group + i + 1) * HEAD_SIZE) for i in range(group)]
        queries_g = jnp.concatenate([qn[:, h] for h in heads], axis=0)
        grads_g = jnp.concatenate([da[:, h] for h in heads], axis=0)
        scores = rowwise_dot(keys_g, queries_g)
        dprobs = rowwise_dot(values_g, grads_g)
        probs, low = [], []
        for i in range(group):
            s = jnp.where(visible, scores[:, i * tok : (i + 1) * tok] * scale_ref[g * group + i], -1e30)
            weights = jnp.where(visible, jnp.exp(s - jnp.max(s, axis=0, keepdims=True)), 0.0)
            p = weights * (1.0 / jnp.sum(weights, axis=0, keepdims=True))
            probs.append(p)
            low.append(p.astype(jnp.bfloat16))
        low_g = jnp.concatenate(low, axis=1)
        attn_t = transposed_dot(values_g, low_g)
        delta = jnp.sum(grads_g.astype(jnp.float32).T * attn_t, axis=0, keepdims=True)
        ds = []
        for i in range(group):
            cols = slice(i * tok, (i + 1) * tok)
            ds.append((scale_ref[g * group + i] * probs[i] * (dprobs[:, cols] - delta[:, cols])).astype(jnp.bfloat16))
        ds_g = jnp.concatenate(ds, axis=1)
        dq_g = transposed_dot(keys_g, ds_g).T
        attn_g = attn_t.T
        for i in range(group):
            attn[:, heads[i]] = attn_g[i * tok : (i + 1) * tok].astype(jnp.bfloat16)
            dq[:, heads[i]] = dq_g[i * tok : (i + 1) * tok]
        dkeys = plain_dot(ds_g, queries_g).reshape(4, tok, HEAD_SIZE)
        dvalues = plain_dot(low_g, grads_g).reshape(4, tok, HEAD_SIZE)
        dkv_own[u, :, lanes] = dkeys[0]
        dkv_own[u, :, value_lanes] = dvalues[0]
        for j in (1, 2, 3):
            dkv_out[u, j - 1, :, lanes] = dkeys[j].astype(jnp.bfloat16)
            dkv_out[u, j - 1, :, value_lanes] = dvalues[j].astype(jnp.bfloat16)
        if g % 2 == 1:
            for j in (3, 2, 1):
                dkv_copies.append(push(dkv_out.at[u, j - 1], dkv_in.at[u, j - 1], dkv_send.at[u, j - 1], dkv_got.at[u, j - 1], along(-j)))
    half = key_start // 2

    def half_of(start, amount, which):
        return pl.ds(pl.multiple_of(start + which * amount, 128), amount)

    attn_copy = pair(3, attn.at[:, half_of(0, half, 1 - core)], attn_pair.at[core])
    attn_pair[core] = attn[:, half_of(0, half, core)]

    def pull(at, g):
        scale = heads_inv[:, at : at + 128]
        x = qk_ref[:, at : at + 128] * scale
        return (scale * (g - x * (half_sums(g * x) / HEAD_SIZE))).astype(jnp.bfloat16)

    for at in range(0, key_start, 128):
        dqkv[:, at : at + 128] = pull(at, dq[:, at : at + 128])
    dq_copy = pair(4, dqkv.at[:, half_of(0, half, 1 - core)], dq_pair.at[core])
    dq_pair[core] = dqkv[:, half_of(0, half, core)]

    rc = 2 * rows
    coords = [(own_x, own_y), (own_y, own_x)]
    partners = [[beside(1, 0), beside(0, 2)], [beside(0, 2), beside(1, 0)]]
    part_copies = [None] * count
    z_copies = [None] * count
    finals = []
    starts = [sum(w for _, _, w in parts[:p]) for p in range(count)]

    def begin(members, left, right):
        product = transposed_dot(left.reshape(2 * tok, width), right).astype(jnp.bfloat16)
        at = 0
        for p in members:
            order, w = parts[p][1:]
            for a in range(2):
                for b in range(2):
                    for r in range(nz):
                        row = ((r * 2 + a) * 2 + b) * rc
                        piece = product[row : row + rc, at : at + w]
                        if order == 0:
                            first[p][a, r, b] = piece
                        else:
                            first[p][b, r, a] = piece
            at += w
            mine = coords[order][0]
            part_copies[p] = push(first[p].at[1 - mine], got_a[p], part_send.at[p, 0], part_got.at[p, 0], partners[order][0])

    def middle(p):
        order = parts[p][1]
        mine, then = coords[order]
        part_copies[p].wait()
        for r in range(nz):
            total = first[p][mine, r, 1 - then].astype(jnp.float32) + got_a[p][r, 1 - then].astype(jnp.float32)
            send_b[p][r] = total.astype(jnp.bfloat16)
        part_copies[p] = push(send_b[p], got_b[p], part_send.at[p, 1], part_got.at[p, 1], partners[order][1])

    def plane_total(p, r):
        mine, then = coords[parts[p][1]]
        near = first[p][mine, r, then].astype(jnp.float32) + got_a[p][r, then].astype(jnp.float32)
        return near + got_b[p][r].astype(jnp.float32)

    def across(p):
        part_copies[p].wait()
        for r in range(nz):
            send_z[p][r] = plane_total(p, r).astype(jnp.bfloat16)
        z_copies[p] = [
            push(send_z[p].at[(own_z + k) % nz], got_z[p].at[k - 1], z_send.at[p, k - 1], z_got.at[p, k - 1], level(k))
            for k in range(1, nz)
        ]

    def finish(p):
        for copy in z_copies[p]:
            copy.wait()
        total = plane_total(p, own_z)
        for k in range(nz - 1):
            total = total + got_z[p][k].astype(jnp.float32)
        cols = slice(starts[p], starts[p] + parts[p][2])
        final[0, :, cols] = total[:rows]
        final[1, :, cols] = total[rows:]
        finals.append(push(final.at[1 - core, :, cols], final_recv.at[:, cols], final_send.at[p], final_got.at[p], other_core))

    of_out, of_query, of_key = [[p for p in range(count) if parts[p][0] == m] for m in range(3)]
    attn_copy.wait()
    grad_copy.wait()
    begin(of_out, grad_pair[...], attn_pair[...].reshape(2 * tok, half))
    dq_copy.wait()
    hidden_copy.wait()
    begin(of_query, hidden_pair[...], dq_pair[...].reshape(2 * tok, half))

    passed = []
    for slot, (i, j) in enumerate(((0, 2), (1, 0), (1, 2))):
        tile_copies[slot].wait()
        where = image.at[(own_x + i) % 2, pl.ds(pl.multiple_of((own_grid + j) % grid_count * tok, tok), tok)]
        passed.append(push(where, where, pass_send.at[slot], pass_got.at[slot], other_core))

    for copy in dkv_copies:
        copy.wait()
    for u in range(span // 128):
        total_kv = dkv_own[u]
        for j in range(3):
            total_kv = total_kv + dkv_in[u, j].astype(jnp.float32)
        at = key_start + u * 128
        dqkv[:, at : at + 128] = pull(at, total_kv[:, :128])
        dqkv[:, at + span : at + span + 128] = total_kv[:, 128:].astype(jnp.bfloat16)
    dkv_copy = pair(5, dqkv.at[:, half_of(key_start, span, 1 - core)], dkv_pair.at[core])
    dkv_pair[core] = dqkv[:, half_of(key_start, span, core)]
    d_hidden = rowwise_dot(dqkv[...], wqkv[...])
    normed = normed_ref[...]
    flow = d_hidden * gain_f
    inner_mean = jnp.sum(flow * normed, axis=1, keepdims=True) / width
    d_tokens = grad_pair[core].astype(jnp.float32) + inv_ref[:, :1] * (flow - normed * inner_mean)
    turned = d_tokens.T
    for c in range(4 * 2):
        pieces = [turned[(r * 8 + c) * rows : (r * 8 + c + 1) * rows] for r in range(nz)]
        tok_out[c] = jnp.concatenate(pieces, axis=0).astype(jnp.bfloat16)
    own_lanes = pl.ds(pl.multiple_of(own_grid * tok, tok), tok)
    gain_own[...] = jnp.sum(d_hidden * normed, axis=0, keepdims=True)
    tok_copies = []
    for slot, (i, j) in enumerate(plane):
        to_grid = (own_grid + j) % grid_count
        goal = (own_x + i) % 2 * grid_count + to_grid
        tok_copies.append(push(tok_out.at[goal], tok_all.at[own_x, :, own_lanes], tok_send.at[slot], tok_got.at[slot], beside(i, j)))
    gain_copies = [
        push(gain_own, gain_got.at[slot], gain_send.at[slot], gain_arrived.at[slot], beside(i, j)) for slot, (i, j) in enumerate(plane)
    ]
    tok_all[own_x, :, own_lanes] = tok_out[own_x * grid_count + own_grid]

    for p in of_out + of_query:
        middle(p)
    dkv_copy.wait()
    begin(of_key, hidden_pair[...], dkv_pair[...].reshape(2 * tok, span))
    tile_pair.wait()
    for copy in passed + tok_copies:
        copy.wait()
    chunks = stem_send.shape[0]
    step = pin // chunks
    stem_copies = []
    for h in range(chunks):
        cols = slice(h * step, (h + 1) * step)
        straight = plain_dot(tok_all[0], image[0, : grid_count * tok, cols]) + plain_dot(tok_all[1], image[1, : grid_count * tok, cols])
        lower = plain_dot(tok_all[0], image[0, halo:, cols]) + plain_dot(tok_all[1], image[1, halo:, cols])
        for r in range(nz):
            both = jnp.concatenate([straight[r * rows : (r + 1) * rows], lower[r * rows : (r + 1) * rows]], axis=0)
            stem_send[h, r] = both.astype(jnp.bfloat16)
        stem_copies.append(
            [
                push(stem_send.at[h, (own_z + k) % nz], stem_got.at[h, k - 1], stem_sent.at[h, k - 1], stem_arrived.at[h, k - 1], level(k))
                for k in range(1, nz)
            ]
        )
    for copy in gain_copies:
        copy.wait()
    gain_sum = gain_own[...]
    for slot in range(len(plane)):
        gain_sum = gain_sum + gain_got[slot]
    gain_plane[...] = gain_sum
    gain_z_copies = [
        push(gain_plane, gain_z.at[k - 1], gain_z_send.at[k - 1], gain_z_got.at[k - 1], level(k)) for k in range(1, nz)
    ]
    for p in of_out + of_query:
        across(p)
    for p in of_key:
        middle(p)
    for p in of_key:
        across(p)
    for p in of_out + of_query:
        finish(p)
    for copy in gain_z_copies:
        copy.wait()
    gain_sum = gain_plane[...]
    for k in range(nz - 1):
        gain_sum = gain_sum + gain_z[k]
    gain_col[...] = jnp.broadcast_to(gain_sum, (128, width)).T
    own_gain = gain_col[pl.ds(pl.multiple_of((own_blk * grid_count + own_grid) * rows, 8), rows), :]
    square = jnp.concatenate([own_gain, jnp.zeros((128 - rows, 128), jnp.float32)], axis=0).T
    gain_out[...] = square[:1, :rows]
    for p in of_key:
        finish(p)
    for h in range(chunks):
        for copy in stem_copies[h]:
            copy.wait()
        total = stem_send[h, own_z].astype(jnp.float32)
        for k in range(nz - 1):
            total = total + stem_got[h, k].astype(jnp.float32)
        cols = slice(h * step, (h + 1) * step)
        stem_out[0, :, cols] = total[:rows]
        stem_out[1, :, cols] = total[rows:]
    for copy in finals:
        copy.wait()
    for source, which in ((final.at[core], core), (final_recv, 1 - core)):
        out_out[:, half_of(0, half, which)] = source[:, :half]
        qkv_out[:, half_of(0, half, which)] = source[:, half : 2 * half]
        qkv_out[:, half_of(key_start, span, which)] = source[:, 2 * half :]


def unpack_kernel(*refs):
    half = len(refs) // 2
    for source, target in zip(refs[:half], refs[half:]):
        target[...] = source[...]


def whole_layer(tiles, grad_out, stem_weight, norm_gain, w_qkv, w_out, per_head_scale, positions):
    blk_count, grid_count = lax.axis_size("blk"), lax.axis_size("grid")
    nz = blk_count // 2
    tok, width = grad_out.shape
    pin = tiles.shape[1]
    qd, span = QUERY_HEADS * HEAD_SIZE, KEY_VALUE_HEADS * HEAD_SIZE
    rows = width // (blk_count * grid_count)
    rc = 2 * rows
    parts = []
    for m, (amount, wide) in enumerate(((qd // 2, 0), (qd // 2, 1), (span, 0))):
        large = (amount // 128 + 1) // 2 * 128
        for order in range(2):
            parts.append((m, order, large if order == wide else amount - large))
    bf, f32 = jnp.bfloat16, jnp.float32
    grouped = [[], [], [], [], [], []]
    for _, _, w in parts:
        grouped[0].append(((2, nz, 2, rc, w), bf))
        grouped[1].append(((nz, 2, rc, w), bf))
        grouped[2].append(((nz, rc, w), bf))
        grouped[3].append(((nz, rc, w), bf))
        grouped[4].append(((nz, rc, w), bf))
        grouped[5].append(((nz - 1, rc, w), bf))
    total = sum(w for _, _, w in parts)
    chunks = 2
    buffers = sum(grouped, []) + [
        ((2, rows, total), f32),
        ((rows, total), f32),
        (stem_weight.shape, bf),
        (w_qkv.shape, bf),
        (w_out.shape, bf),
        ((2, grid_count * tok + TC, pin), bf),
        ((TC, pin), bf),
        ((2, tok, width), bf),
        ((2, tok, width), bf),
        ((2, tok, qd // 2), bf),
        ((2, tok, qd // 2), bf),
        ((2, tok, span), bf),
        ((span // 128, 4, tok, 256), bf),
        ((span // 128, 3, tok, 256), bf),
        ((span // 128, tok, 256), f32),
        ((span // 128, 3, tok, 256), bf),
        ((tok, width), f32),
        ((tok, 128), f32),
        ((tok, qd + span), f32),
        ((tok, qd + span), f32),
        ((tok, qd), bf),
        ((tok, qd), bf),
        ((tok, qd), bf),
        ((tok, qd), f32),
        ((tok, w_qkv.shape[1]), bf),
        ((2 * grid_count, nz * rows, tok), bf),
        ((2, nz * rows, grid_count * tok), bf),
        ((chunks, nz, rc, pin // chunks), bf),
        ((chunks, nz - 1, rc, pin // chunks), bf),
        ((1, width), f32),
        ((2 * grid_count - 1, 1, width), f32),
        ((1, width), f32),
        ((nz - 1, 1, width), f32),
        ((width, 128), f32),
    ]
    dma = pltpu.SemaphoreType.DMA
    halves, count, others = span // 128, len(parts), 2 * grid_count - 1
    semaphores = [dma((6,)), dma((6,)), dma((6,)), dma((count,)), dma((count,)), dma, dma, dma((3,)), dma((3,)), dma((3,)), dma((3,))]
    semaphores += [dma((halves, 4)), dma((halves, 4)), dma((halves, 3)), dma((halves, 3)), dma((count, 2)), dma((count, 2))]
    semaphores += [dma((count, nz - 1)), dma((count, nz - 1)), dma((others,)), dma((others,)), dma((others,)), dma((others,))]
    semaphores += [dma((nz - 1,)), dma((nz - 1,)), dma((chunks, nz - 1)), dma((chunks, nz - 1))]
    vmem = pl.BlockSpec(memory_space=pltpu.VMEM)
    hbm = pl.BlockSpec(memory_space=pl.ANY)
    shapes = [
        jax.ShapeDtypeStruct(shape, f32)
        for shape in ((2, rows, pin), (1, rows), (rows, w_qkv.shape[1]), (rows, qd))
    ]
    results = pl.pallas_call(
        partial(layer_kernel, (nz, parts)),
        out_shape=shapes,
        in_specs=[pl.BlockSpec(memory_space=pltpu.SMEM), hbm, hbm, hbm, vmem, hbm, hbm, vmem],
        out_specs=[vmem] * 4,
        scratch_shapes=[pltpu.VMEM(shape, kind) for shape, kind in buffers] + semaphores,
        compiler_params=pltpu.CompilerParams(collective_id=0, has_side_effects=True, vmem_limit_bytes=63000000),
    )(per_head_scale, tiles, grad_out, stem_weight, norm_gain, w_qkv, w_out, positions.reshape(-1, tok))
    return pl.pallas_call(unpack_kernel, out_shape=shapes, in_specs=[vmem] * 4, out_specs=[vmem] * 4)(*results)


def shards(patches, stem_weight, norm_gain, w_qkv, w_out, per_head_scale, positions, d_out):
    tiles = patches[0]
    grad_out = d_out[0]
    if fits_planes(grad_out.shape[1]):
        d_stem, d_gain, d_qkv, d_out_t = whole_layer(
            tiles, grad_out, stem_weight, norm_gain, w_qkv, w_out, per_head_scale, positions
        )
        return (d_stem.transpose(0, 2, 1), d_gain.reshape(-1), d_qkv, d_out_t.T)
    token_rows = tiles.shape[0]
    group_factor = QUERY_HEADS // KEY_VALUE_HEADS
    query_span_width = QUERY_HEADS * HEAD_SIZE
    key_span_width = KEY_VALUE_HEADS * HEAD_SIZE
    arrived = shifted(tiles[:TC], "grid", -1)
    below = jnp.concatenate([tiles[TC:], arrived], axis=0)
    stem = jnp.dot(tiles, stem_weight[0], preferred_element_type=jnp.float32)
    stem = stem + jnp.dot(below, stem_weight[1], preferred_element_type=jnp.float32)
    token_f = lax.optimization_barrier(stem.astype(jnp.bfloat16)).astype(jnp.float32)
    gain_f = norm_gain.astype(jnp.float32)
    normed = row_norm(token_f)
    hidden = (normed * gain_f).astype(jnp.bfloat16)
    query_key_value = jnp.dot(hidden, w_qkv, preferred_element_type=jnp.float32)
    query = query_key_value[:, :query_span_width].reshape(token_rows, QUERY_HEADS, HEAD_SIZE)
    key = query_key_value[:, query_span_width : query_span_width + key_span_width].reshape(
        token_rows, KEY_VALUE_HEADS, HEAD_SIZE
    )
    query_normalized = head_norm(query).astype(jnp.bfloat16)
    key_n = head_norm(key).astype(jnp.bfloat16).reshape(token_rows, key_span_width)
    value = query_key_value[:, query_span_width + key_span_width :].astype(jnp.bfloat16)
    attention_gradient = jnp.dot(grad_out, w_out.T, preferred_element_type=jnp.float32).astype(
        jnp.bfloat16
    )
    kv_own = jnp.concatenate([key_n, value], axis=1)
    blk_count = lax.axis_size("blk")
    own_index = lax.axis_index("blk")
    blocks = [kv_own]
    for offset in range(1, 4):
        blocks.append(passed_along(kv_own, "blk", offset))
    causal_window = jnp.concatenate(blocks, axis=0)
    key_pos = jnp.concatenate(
        [
            lax.dynamic_slice_in_dim(
                positions, (own_index - offset) % blk_count * token_rows, token_rows
            )
            for offset in range(4)
        ]
    )
    query_pos = lax.dynamic_slice_in_dim(positions, own_index * token_rows, token_rows)
    visible = (key_pos[None, :] <= query_pos[:, None])[None]
    every_key = causal_window.shape[0]
    query_cube = query_normalized.reshape(token_rows, KEY_VALUE_HEADS, group_factor, HEAD_SIZE)
    gradient_cube = attention_gradient.reshape(token_rows, KEY_VALUE_HEADS, group_factor, HEAD_SIZE)
    key_cube = causal_window[:, :key_span_width].reshape(every_key, KEY_VALUE_HEADS, HEAD_SIZE)
    value_cube = causal_window[:, key_span_width:].reshape(every_key, KEY_VALUE_HEADS, HEAD_SIZE)
    score_scales = per_head_scale.reshape(KEY_VALUE_HEADS, group_factor)
    prob_list = []
    low_list = []
    attn_list = []
    for query_head_group in range(KEY_VALUE_HEADS):
        scale_col = score_scales[query_head_group][:, None, None]
        attention_scores = (
            jnp.einsum(
                "trd,sd->rts",
                query_cube[:, query_head_group],
                key_cube[:, query_head_group],
                preferred_element_type=jnp.float32,
            )
            * scale_col
        )
        attention_scores = jnp.where(visible, attention_scores, -1e30)
        top = jnp.max(attention_scores, axis=-1, keepdims=True)
        weights = jnp.where(visible, jnp.exp(attention_scores - top), 0.0)
        probs = weights / jnp.sum(weights, axis=-1, keepdims=True)
        probability_narrow = probs.astype(jnp.bfloat16)
        prob_list.append(probs)
        low_list.append(probability_narrow)
        attn_list.append(
            jnp.einsum(
                "rts,sd->trd",
                probability_narrow,
                value_cube[:, query_head_group],
                preferred_element_type=jnp.float32,
            )
        )
    attention_output = (
        jnp.stack(attn_list, axis=1).reshape(token_rows, query_span_width).astype(jnp.bfloat16)
    )
    dquery_list = []
    dkey_list = []
    dvalue_list = []
    for query_head_group in range(KEY_VALUE_HEADS):
        scale_col = score_scales[query_head_group][:, None, None]
        grad_group = gradient_cube[:, query_head_group]
        softmax_delta = jnp.sum(
            grad_group.astype(jnp.float32) * attn_list[query_head_group], axis=-1
        )
        probability_gradient = jnp.einsum(
            "trd,sd->rts",
            grad_group,
            value_cube[:, query_head_group],
            preferred_element_type=jnp.float32,
        )
        score_gradient = (
            scale_col
            * prob_list[query_head_group]
            * (probability_gradient - softmax_delta.T[:, :, None])
        ).astype(jnp.bfloat16)
        dquery_list.append(
            jnp.einsum(
                "rts,sd->trd",
                score_gradient,
                key_cube[:, query_head_group],
                preferred_element_type=jnp.float32,
            )
        )
        dkey_list.append(
            jnp.einsum(
                "rts,trd->sd",
                score_gradient,
                query_cube[:, query_head_group],
                preferred_element_type=jnp.float32,
            )
        )
        dvalue_list.append(
            jnp.einsum(
                "rts,trd->sd",
                low_list[query_head_group],
                grad_group,
                preferred_element_type=jnp.float32,
            )
        )
    query_gradient = jnp.stack(dquery_list, axis=1).reshape(token_rows, QUERY_HEADS, HEAD_SIZE)
    dkey_all = jnp.stack(dkey_list, axis=1).reshape(every_key, key_span_width)
    dvalue_all = jnp.stack(dvalue_list, axis=1).reshape(every_key, key_span_width)
    partial_terms = jnp.concatenate([dkey_all, dvalue_all], axis=1)
    pieces = [partial_terms[offset * token_rows : (offset + 1) * token_rows] for offset in range(4)]
    carried_state = pieces[0]
    for offset in (1, 2, 3):
        carried_state = carried_state + passed_along(pieces[offset], "blk", -offset)
    pull_query = jax.vjp(head_norm, query)[1]
    gather_key = jax.vjp(head_norm, key)[1]
    dq_full = pull_query(query_gradient)[0].reshape(token_rows, query_span_width)
    key_gradient_whole = gather_key(
        carried_state[:, :key_span_width].reshape(token_rows, KEY_VALUE_HEADS, HEAD_SIZE)
    )[0].reshape(token_rows, key_span_width)
    d_qkv = jnp.concatenate(
        [dq_full, key_gradient_whole, carried_state[:, key_span_width:]], axis=1
    ).astype(jnp.bfloat16)
    d_hidden = jnp.dot(d_qkv, w_qkv.T, preferred_element_type=jnp.float32)
    gain_term = jnp.sum(d_hidden * normed, axis=0)
    pull_tokens = jax.vjp(row_norm, token_f)[1]
    d_tokens = (grad_out.astype(jnp.float32) + pull_tokens(d_hidden * gain_f)[0]).astype(
        jnp.bfloat16
    )
    stem_term = jnp.stack(
        [
            jnp.dot(tiles.T, d_tokens, preferred_element_type=jnp.float32),
            jnp.dot(below.T, d_tokens, preferred_element_type=jnp.float32),
        ]
    )
    qkv_term = jnp.dot(hidden.T, d_qkv, preferred_element_type=jnp.float32)
    out_term = jnp.dot(attention_output.T, grad_out, preferred_element_type=jnp.float32)
    d_stem_weight = lax.psum_scatter(stem_term, ("blk", "grid"), scatter_dimension=2, tiled=True)
    d_norm_gain = lax.psum_scatter(gain_term, ("blk", "grid"), scatter_dimension=0, tiled=True)
    d_w_qkv = lax.psum_scatter(qkv_term, ("blk", "grid"), scatter_dimension=0, tiled=True)
    d_w_out = lax.psum_scatter(out_term, ("blk", "grid"), scatter_dimension=1, tiled=True)
    return (d_stem_weight, d_norm_gain, d_w_qkv, d_w_out)


def solution(mesh):
    placed = (P("grid", "blk", None), P(), P(), P(), P(), P(), P(), P("grid", "blk", None))
    return jax.shard_map(
        shards,
        mesh=mesh,
        in_specs=placed,
        out_specs=(
            P(None, None, ("blk", "grid")),
            P(("blk", "grid")),
            P(("blk", "grid"), None),
            P(None, ("blk", "grid")),
        ),
        check_vma=False,
    )
```

```python
from functools import partial

import jax
import jax.numpy as jnp
from jax import lax
from jax.experimental import pallas as pl
from jax.experimental.pallas import tpu as pltpu
from jax.sharding import PartitionSpec as P

QUERY_HEADS = 12
KEY_VALUE_HEADS = 4
HEAD_SIZE = 64
TC = 16


def shifted(x, axis, by):
    peers = lax.axis_size(axis)
    pairs = [(i, i + by) for i in range(peers) if 0 <= i + by < peers]
    return lax.ppermute(x, axis, pairs)


def passed_along(x, axis, by):
    peers = lax.axis_size(axis)
    return lax.ppermute(x, axis, [(i, (i + by) % peers) for i in range(peers)])


def row_norm(values):
    return values * lax.rsqrt(jnp.mean(values * values, axis=-1, keepdims=True) + 1e-05)


def head_norm(values):
    return values * lax.rsqrt(jnp.mean(values * values, axis=-1, keepdims=True) + 1e-06)


def transposed_dot(a, b):
    return lax.dot_general(a, b, (((0,), (0,)), ((), ())), preferred_element_type=jnp.float32)


def rowwise_dot(a, b):
    return lax.dot_general(a, b, (((1,), (1,)), ((), ())), preferred_element_type=jnp.float32)


def plain_dot(a, b):
    return jnp.dot(a, b, preferred_element_type=jnp.float32)


def half_sums(x):
    low = lax.broadcasted_iota(jnp.int32, x.shape, 1) < HEAD_SIZE
    first = jnp.sum(jnp.where(low, x, 0.0), axis=1, keepdims=True)
    second = jnp.sum(jnp.where(low, 0.0, x), axis=1, keepdims=True)
    return jnp.where(low, first, second)


def fits_planes(width):
    blocks, bands = lax.axis_size("blk"), lax.axis_size("grid")
    devices = blocks * bands
    return bands == 4 and blocks == 8 and width % devices == 0 and (width // devices) % 8 == 0


def layer_kernel(plan, *refs):
    nz, parts = plan
    (scale_ref, tiles_hbm, grad_hbm, stem_hbm, gain_ref, wqkv_hbm, wout_hbm, pos_ref) = refs[:8]
    (stem_out, gain_out, qkv_out, out_out) = refs[8:12]
    scratch = list(refs[12:])
    count = len(parts)
    first = [scratch.pop(0) for _ in range(count)]
    got_a = [scratch.pop(0) for _ in range(count)]
    send_b = [scratch.pop(0) for _ in range(count)]
    got_b = [scratch.pop(0) for _ in range(count)]
    send_z = [scratch.pop(0) for _ in range(count)]
    got_z = [scratch.pop(0) for _ in range(count)]
    send_w = [scratch.pop(0) for _ in range(count)]
    got_w = [scratch.pop(0) for _ in range(count)]
    (final, final_recv, stem_w, wqkv, wout, image, halo_rows, grad_pair, hidden_pair, attn_pair, dq_pair, dkv_pair,
     kv, dkv_out, dkv_own, dkv_in, dkv_mid, normed_ref, inv_ref, qk_ref, heads_inv, qn, da, attn, dq, dqkv,
     tok_out, tok_all, stem_send, stem_got, stem_next, stem_last, gain_own, gain_got, gain_plane, gain_z, gain_col,
     load_sem, pair_send, pair_got, final_send, final_got, halo_send, halo_got, tile_send, tile_got, pass_send, pass_got,
     kv_send, kv_got, dkv_send, dkv_got, part_send, part_got, z_send, z_got, tok_send, tok_got, gain_send, gain_arrived,
     gain_z_send, gain_z_got, stem_sent, stem_arrived) = scratch
    tok, width = grad_pair.shape[1:]
    halo = halo_rows.shape[0]
    pin = image.shape[2]
    span = kv.shape[0] * 128
    group = QUERY_HEADS // KEY_VALUE_HEADS
    own_blk = lax.axis_index("blk")
    own_grid = lax.axis_index("grid")
    blk_count = lax.axis_size("blk")
    grid_count = lax.axis_size("grid")
    core = own_grid % 2
    own_y = own_grid // 2
    own_x = own_blk % 2
    own_z = own_blk // 2
    z_low, z_high = own_z % 2, own_z // 2
    rows = width // (blk_count * grid_count)
    other_core = {"blk": own_blk, "grid": own_grid + 1 - 2 * core}
    above = {"blk": own_blk, "grid": (own_grid + grid_count - 1) % grid_count}
    plane = [(i, j) for i in range(2) for j in range(grid_count) if i + j > 0]

    def along(offset):
        return {"blk": (own_blk + offset + blk_count) % blk_count, "grid": own_grid}

    def beside(i, j):
        return {"blk": own_z * 2 + (own_x + i) % 2, "grid": (own_grid + j) % grid_count}

    def level(k):
        return {"blk": (own_z + k) % nz * 2 + own_x, "grid": own_grid}

    z_near = {"blk": own_blk + (1 - 2 * z_low) * 2, "grid": own_grid}
    z_far = {"blk": own_blk + (1 - 2 * z_high) * 4, "grid": own_grid}

    own_rows = pl.ds(pl.multiple_of(own_grid * tok, tok), tok)
    loads = [
        pltpu.make_async_copy(tiles_hbm, image.at[own_x, own_rows], load_sem.at[0]),
        pltpu.make_async_copy(stem_hbm.at[0], stem_w.at[0], load_sem.at[1]),
        pltpu.make_async_copy(stem_hbm.at[1], stem_w.at[1], load_sem.at[2]),
        pltpu.make_async_copy(wqkv_hbm, wqkv, load_sem.at[3]),
        pltpu.make_async_copy(grad_hbm, grad_pair.at[core], load_sem.at[4]),
        pltpu.make_async_copy(wout_hbm, wout, load_sem.at[5]),
    ]
    barrier = pltpu.get_barrier_semaphore()
    peers = [beside(i, j) for i, j in plane] + [level(k) for k in range(1, nz)] + [along(j) for j in (1, 2, 3, -1, -2, -3)]
    for peer in peers:
        pl.semaphore_signal(barrier, inc=1, device_id=peer, device_id_type=pl.DeviceIdType.MESH)
    for load in loads:
        load.start()
    image[:, grid_count * tok :] = jnp.zeros((2, halo, pin), image.dtype)

    def push(source, target, sems, got, device):
        copy = pltpu.make_async_remote_copy(
            src_ref=source, dst_ref=target, send_sem=sems, recv_sem=got, device_id=device, device_id_type=pl.DeviceIdType.MESH
        )
        copy.start()
        return copy

    def pair(which, source, target):
        return push(source, target, pair_send.at[which], pair_got.at[which], other_core)

    def tiles_to(slot, i, j):
        mine = image.at[own_x, own_rows]
        return push(mine, mine, tile_send.at[slot], tile_got.at[slot], beside(i, j))

    loads[0].wait()
    pl.semaphore_wait(barrier, len(peers))
    halo_copy = push(image.at[own_x, pl.ds(pl.multiple_of(own_grid * tok, tok), halo)], halo_rows, halo_send, halo_got, above)
    tile_copies = [tiles_to(0, 0, 2), tiles_to(1, 1, 0)]
    tile_pair = pair(0, image.at[own_x, own_rows], image.at[own_x, own_rows])

    loads[1].wait()
    tiles = image[own_x, own_rows]
    stem = plain_dot(tiles, stem_w[0])
    loads[2].wait()
    halo_copy.wait()

    @pl.when(own_grid == grid_count - 1)
    def _():
        halo_rows[...] = jnp.zeros(halo_rows.shape, halo_rows.dtype)

    below = jnp.concatenate([tiles[halo:], halo_rows[...]], axis=0)
    stem = stem + plain_dot(below, stem_w[1])
    token_f = stem.astype(jnp.bfloat16).astype(jnp.float32)
    inv = lax.rsqrt(jnp.sum(token_f * token_f, axis=1, keepdims=True) / width + 1e-05)
    normed = token_f * inv
    normed_ref[...] = normed
    inv_ref[...] = jnp.broadcast_to(inv, inv_ref.shape)
    gain_f = gain_ref[...].astype(jnp.float32).reshape(1, width)
    hidden = (normed * gain_f).astype(jnp.bfloat16)
    hidden_pair[core] = hidden
    loads[3].wait()
    key_start = QUERY_HEADS * HEAD_SIZE

    def normalize(x):
        scale = lax.rsqrt(half_sums(x * x) / HEAD_SIZE + 1e-06)
        return scale, (x * scale).astype(jnp.bfloat16)

    keys = plain_dot(hidden, wqkv[:, key_start:])
    kv_copies = []
    for u in range(span // 128):
        at = u * 128
        heads_inv[:, key_start + at : key_start + at + 128], kv[u, 0, :, :128] = normalize(keys[:, at : at + 128])
        kv[u, 0, :, 128:] = keys[:, span + at : span + at + 128].astype(jnp.bfloat16)
        kv_copies.append([push(kv.at[u, 0], kv.at[u, 2], kv_send.at[u, 0], kv_got.at[u, 2], along(2))])
        slot = 1 + 2 * own_x
        kv_copies[u].append(push(kv.at[u, 0], kv.at[u, slot], kv_send.at[u, 1], kv_got.at[u, slot], along(slot)))
    qk_ref[:, key_start:] = keys[:, :span]
    loads[4].wait()
    grad_copy = pair(1, grad_pair.at[core], grad_pair.at[core])
    hidden_copy = pair(2, hidden_pair.at[core], hidden_pair.at[core])
    queries = plain_dot(hidden, wqkv[:, :key_start])
    qk_ref[:, :key_start] = queries
    for at in range(0, key_start, 128):
        heads_inv[:, at : at + 128], qn[:, at : at + 128] = normalize(queries[:, at : at + 128])
    loads[5].wait()
    grad_own = grad_pair[core]
    da[...] = rowwise_dot(grad_own, wout[...]).astype(jnp.bfloat16)

    query_pos = pos_ref[pl.ds(own_blk, 1), :]
    seen = []
    for j in range(4):
        key_pos = pos_ref[pl.ds((own_blk + blk_count - j) % blk_count, 1), :]
        column = jnp.broadcast_to(key_pos, (tok, tok)).T
        seen.append(column <= query_pos)
    visible = jnp.concatenate([jnp.where(x, 1.0, 0.0) for x in seen], axis=0) > 0.5
    for u in range(span // 128):
        kv_copies[u][0].wait_recv()
        slot = 3 - 2 * own_x
        kv_copies[u].append(push(kv.at[u, 2], kv.at[u, slot], kv_send.at[u, 2], kv_got.at[u, slot], beside(1, 0)))

    def combine(u):
        side_copies[u].wait()
        dkv_mid[u] = (dkv_out[u, 1].astype(jnp.float32) + dkv_in[u, 1].astype(jnp.float32)).astype(jnp.bfloat16)
        dkv_copies.append(push(dkv_mid.at[u], dkv_in.at[u, 2], dkv_send.at[u, 2], dkv_got.at[u, 2], along(-2)))

    dkv_copies, side_copies = [], []
    for g in range(KEY_VALUE_HEADS):
        u, low_lane = g // 2, g % 2 * HEAD_SIZE
        lanes = slice(low_lane, low_lane + HEAD_SIZE)
        value_lanes = slice(128 + low_lane, 128 + low_lane + HEAD_SIZE)
        if g % 2 == 0:
            kv_copies[u][0].wait_send()
            for copy in kv_copies[u][1:]:
                copy.wait()
        if g == 2:
            tile_copies[1].wait()
            near = image.at[1 - own_x, own_rows]
            tile_copies.append(push(near, near, tile_send.at[2], tile_got.at[2], beside(0, 2)))
        keys_g = kv[u, :, :, lanes].reshape(4 * tok, HEAD_SIZE)
        values_g = kv[u, :, :, value_lanes].reshape(4 * tok, HEAD_SIZE)
        heads = [slice((g * group + i) * HEAD_SIZE, (g * group + i + 1) * HEAD_SIZE) for i in range(group)]
        queries_g = jnp.concatenate([qn[:, h] for h in heads], axis=0)
        grads_g = jnp.concatenate([da[:, h] for h in heads], axis=0)
        scores = rowwise_dot(keys_g, queries_g)
        dprobs = rowwise_dot(values_g, grads_g)
        probs, low = [], []
        for i in range(group):
            s = jnp.where(visible, scores[:, i * tok : (i + 1) * tok] * scale_ref[g * group + i], -1e30)
            weights = jnp.where(visible, jnp.exp(s - jnp.max(s, axis=0, keepdims=True)), 0.0)
            p = weights * (1.0 / jnp.sum(weights, axis=0, keepdims=True))
            probs.append(p)
            low.append(p.astype(jnp.bfloat16))
        low_g = jnp.concatenate(low, axis=1)
        attn_t = transposed_dot(values_g, low_g)
        delta = jnp.sum(grads_g.astype(jnp.float32).T * attn_t, axis=0, keepdims=True)
        ds = []
        for i in range(group):
            cols = slice(i * tok, (i + 1) * tok)
            ds.append((scale_ref[g * group + i] * probs[i] * (dprobs[:, cols] - delta[:, cols])).astype(jnp.bfloat16))
        ds_g = jnp.concatenate(ds, axis=1)
        dq_g = transposed_dot(keys_g, ds_g).T
        attn_g = attn_t.T
        for i in range(group):
            attn[:, heads[i]] = attn_g[i * tok : (i + 1) * tok].astype(jnp.bfloat16)
            dq[:, heads[i]] = dq_g[i * tok : (i + 1) * tok]
        dkeys = plain_dot(ds_g, queries_g).reshape(4, tok, HEAD_SIZE)
        dvalues = plain_dot(low_g, grads_g).reshape(4, tok, HEAD_SIZE)
        dkv_own[u, :, lanes] = dkeys[0]
        dkv_own[u, :, value_lanes] = dvalues[0]
        for j in (1, 2, 3):
            dkv_out[u, j - 1, :, lanes] = dkeys[j].astype(jnp.bfloat16)
            dkv_out[u, j - 1, :, value_lanes] = dvalues[j].astype(jnp.bfloat16)
        if g % 2 == 1:
            side_copies.append(push(dkv_out.at[u, 2 * own_x], dkv_in.at[u, 1], dkv_send.at[u, 1], dkv_got.at[u, 1], beside(1, 0)))
            direct = dkv_out.at[u, 2 - 2 * own_x]
            dkv_copies.append(push(direct, dkv_in.at[u, 0], dkv_send.at[u, 0], dkv_got.at[u, 0], along(2 * own_x - 3)))
        if g == 2:
            combine(0)
    half = key_start // 2

    def half_of(start, amount, which):
        return pl.ds(pl.multiple_of(start + which * amount, 128), amount)

    attn_copy = pair(3, attn.at[:, half_of(0, half, 1 - core)], attn_pair.at[core])
    attn_pair[core] = attn[:, half_of(0, half, core)]

    def pull(at, g):
        scale = heads_inv[:, at : at + 128]
        x = qk_ref[:, at : at + 128] * scale
        return (scale * (g - x * (half_sums(g * x) / HEAD_SIZE))).astype(jnp.bfloat16)

    for at in range(0, key_start, 128):
        dqkv[:, at : at + 128] = pull(at, dq[:, at : at + 128])
    dq_copy = pair(4, dqkv.at[:, half_of(0, half, 1 - core)], dq_pair.at[core])
    dq_pair[core] = dqkv[:, half_of(0, half, core)]

    rc = 2 * rows
    coords = [(own_x, own_y), (own_y, own_x)]
    partners = [[beside(1, 0), beside(0, 2)], [beside(0, 2), beside(1, 0)]]
    part_copies = [None] * count
    finals = []
    starts = [sum(w for _, _, w in parts[:p]) for p in range(count)]

    def begin(members, left, right):
        product = transposed_dot(left.reshape(2 * tok, width), right).astype(jnp.bfloat16)
        at = 0
        for p in members:
            order, w = parts[p][1:]
            for a in range(2):
                for b in range(2):
                    for r in range(nz):
                        row = ((r * 2 + a) * 2 + b) * rc
                        piece = product[row : row + rc, at : at + w]
                        if order == 0:
                            first[p][a, r, b] = piece
                        else:
                            first[p][b, r, a] = piece
            at += w
            mine = coords[order][0]
            part_copies[p] = push(first[p].at[1 - mine], got_a[p], part_send.at[p, 0], part_got.at[p, 0], partners[order][0])

    def middle(p):
        order = parts[p][1]
        mine, then = coords[order]
        part_copies[p].wait()
        for r in range(nz):
            total = first[p][mine, r, 1 - then].astype(jnp.float32) + got_a[p][r, 1 - then].astype(jnp.float32)
            send_b[p][r] = total.astype(jnp.bfloat16)
        part_copies[p] = push(send_b[p], got_b[p], part_send.at[p, 1], part_got.at[p, 1], partners[order][1])

    def plane_total(p, r):
        mine, then = coords[parts[p][1]]
        near = first[p][mine, r, then].astype(jnp.float32) + got_a[p][r, then].astype(jnp.float32)
        return near + got_b[p][r].astype(jnp.float32)

    def across(p):
        part_copies[p].wait()
        for h in range(2):
            send_z[p][h] = plane_total(p, 2 * h + 1 - z_low).astype(jnp.bfloat16)
        part_copies[p] = push(send_z[p], got_z[p], z_send.at[p, 0], z_got.at[p, 0], z_near)

    def near_total(p, h):
        return plane_total(p, 2 * h + z_low) + got_z[p][h].astype(jnp.float32)

    def beyond(p):
        part_copies[p].wait()
        send_w[p][...] = near_total(p, 1 - z_high).astype(jnp.bfloat16)
        part_copies[p] = push(send_w[p], got_w[p], z_send.at[p, 1], z_got.at[p, 1], z_far)

    def finish(p):
        part_copies[p].wait()
        total = near_total(p, z_high) + got_w[p][...].astype(jnp.float32)
        cols = slice(starts[p], starts[p] + parts[p][2])
        final[0, :, cols] = total[:rows]
        final[1, :, cols] = total[rows:]
        finals.append(push(final.at[1 - core, :, cols], final_recv.at[:, cols], final_send.at[p], final_got.at[p], other_core))

    combine(1)
    of_out, of_query, of_key = [[p for p in range(count) if parts[p][0] == m] for m in range(3)]
    attn_copy.wait()
    grad_copy.wait()
    begin(of_out, grad_pair[...], attn_pair[...].reshape(2 * tok, half))
    dq_copy.wait()
    hidden_copy.wait()
    begin(of_query, hidden_pair[...], dq_pair[...].reshape(2 * tok, half))

    for p in of_out:
        middle(p)
    passed = []
    for slot, (i, j) in enumerate(((0, 2), (1, 0), (1, 2))):
        if slot != 1:
            tile_copies[slot].wait()
        where = image.at[(own_x + i) % 2, pl.ds(pl.multiple_of((own_grid + j) % grid_count * tok, tok), tok)]
        passed.append(push(where, where, pass_send.at[slot], pass_got.at[slot], other_core))

    for copy in dkv_copies:
        copy.wait()
    for u in range(span // 128):
        total_kv = dkv_own[u]
        for j in (0, 2):
            total_kv = total_kv + dkv_in[u, j].astype(jnp.float32)
        at = key_start + u * 128
        dqkv[:, at : at + 128] = pull(at, total_kv[:, :128])
        dqkv[:, at + span : at + span + 128] = total_kv[:, 128:].astype(jnp.bfloat16)
    dkv_copy = pair(5, dqkv.at[:, half_of(key_start, span, 1 - core)], dkv_pair.at[core])
    dkv_pair[core] = dqkv[:, half_of(key_start, span, core)]
    d_hidden = rowwise_dot(dqkv[...], wqkv[...])
    normed = normed_ref[...]
    flow = d_hidden * gain_f
    inner_mean = jnp.sum(flow * normed, axis=1, keepdims=True) / width
    d_tokens = grad_pair[core].astype(jnp.float32) + inv_ref[:, :1] * (flow - normed * inner_mean)
    turned = d_tokens.T
    for c in range(4 * 2):
        pieces = [turned[(r * 8 + c) * rows : (r * 8 + c + 1) * rows] for r in range(nz)]
        tok_out[c] = jnp.concatenate(pieces, axis=0).astype(jnp.bfloat16)
    own_lanes = pl.ds(pl.multiple_of(own_grid * tok, tok), tok)
    gain_own[...] = jnp.sum(d_hidden * normed, axis=0, keepdims=True)
    tok_copies = []
    for slot, (i, j) in enumerate(plane):
        to_grid = (own_grid + j) % grid_count
        goal = (own_x + i) % 2 * grid_count + to_grid
        tok_copies.append(push(tok_out.at[goal], tok_all.at[own_x, :, own_lanes], tok_send.at[slot], tok_got.at[slot], beside(i, j)))
    gain_copies = [
        push(gain_own, gain_got.at[slot], gain_send.at[slot], gain_arrived.at[slot], beside(i, j)) for slot, (i, j) in enumerate(plane)
    ]
    tok_all[own_x, :, own_lanes] = tok_out[own_x * grid_count + own_grid]

    for p in of_out:
        across(p)
    for p in of_query:
        middle(p)
    dkv_copy.wait()
    begin(of_key, hidden_pair[...], dkv_pair[...].reshape(2 * tok, span))
    tile_pair.wait()
    for copy in passed + tok_copies:
        copy.wait()
    chunks = stem_send.shape[0]
    step = pin // chunks
    stem_copies = []
    for h in range(chunks):
        cols = slice(h * step, (h + 1) * step)
        straight = plain_dot(tok_all[0], image[0, : grid_count * tok, cols]) + plain_dot(tok_all[1], image[1, : grid_count * tok, cols])
        lower = plain_dot(tok_all[0], image[0, halo:, cols]) + plain_dot(tok_all[1], image[1, halo:, cols])
        for r in range(nz):
            both = jnp.concatenate([straight[r * rows : (r + 1) * rows], lower[r * rows : (r + 1) * rows]], axis=0)
            stem_send[h, r % 2, r // 2] = both.astype(jnp.bfloat16)
        stem_copies.append(push(stem_send.at[h, 1 - z_low], stem_got.at[h], stem_sent.at[h, 0], stem_arrived.at[h, 0], z_near))

    def stem_near(h, k):
        return stem_send[h, z_low, k].astype(jnp.float32) + stem_got[h, k].astype(jnp.float32)

    def stem_beyond(h):
        stem_copies[h].wait()
        stem_next[h] = stem_near(h, 1 - z_high).astype(jnp.bfloat16)
        stem_copies[h] = push(stem_next.at[h], stem_last.at[h], stem_sent.at[h, 1], stem_arrived.at[h, 1], z_far)

    for copy in gain_copies:
        copy.wait()
    gain_sum = gain_own[...]
    for slot in range(len(plane)):
        gain_sum = gain_sum + gain_got[slot]
    gain_plane[...] = gain_sum
    gain_z_copies = [
        push(gain_plane, gain_z.at[k - 1], gain_z_send.at[k - 1], gain_z_got.at[k - 1], level(k)) for k in range(1, nz)
    ]
    for p in of_query:
        across(p)
    for p in of_out:
        beyond(p)
    for p in of_key:
        middle(p)
    for h in range(chunks):
        stem_beyond(h)
    for p in of_key:
        across(p)
    for p in of_query:
        beyond(p)
    for p in of_key:
        beyond(p)
    for p in of_out + of_query:
        finish(p)
    for copy in gain_z_copies:
        copy.wait()
    gain_sum = gain_plane[...]
    for k in range(nz - 1):
        gain_sum = gain_sum + gain_z[k]
    gain_col[...] = jnp.broadcast_to(gain_sum, (128, width)).T
    own_gain = gain_col[pl.ds(pl.multiple_of((own_blk * grid_count + own_grid) * rows, 8), rows), :]
    square = jnp.concatenate([own_gain, jnp.zeros((128 - rows, 128), jnp.float32)], axis=0).T
    gain_out[...] = square[:1, :rows]
    for p in of_key:
        finish(p)
    for h in range(chunks):
        stem_copies[h].wait()
        total = stem_near(h, z_high) + stem_last[h].astype(jnp.float32)
        cols = slice(h * step, (h + 1) * step)
        stem_out[0, :, cols] = total[:rows]
        stem_out[1, :, cols] = total[rows:]
    for copy in finals:
        copy.wait()
    for source, which in ((final.at[core], core), (final_recv, 1 - core)):
        out_out[:, half_of(0, half, which)] = source[:, :half]
        qkv_out[:, half_of(0, half, which)] = source[:, half : 2 * half]
        qkv_out[:, half_of(key_start, span, which)] = source[:, 2 * half :]


def unpack_kernel(*refs):
    half = len(refs) // 2
    for source, target in zip(refs[:half], refs[half:]):
        target[...] = source[...]


def whole_layer(tiles, grad_out, stem_weight, norm_gain, w_qkv, w_out, per_head_scale, positions):
    blk_count, grid_count = lax.axis_size("blk"), lax.axis_size("grid")
    nz = blk_count // 2
    tok, width = grad_out.shape
    pin = tiles.shape[1]
    qd, span = QUERY_HEADS * HEAD_SIZE, KEY_VALUE_HEADS * HEAD_SIZE
    rows = width // (blk_count * grid_count)
    rc = 2 * rows
    parts = []
    for m, (amount, wide) in enumerate(((qd // 2, 0), (qd // 2, 1), (span, 0))):
        large = (amount // 128 + 1) // 2 * 128
        for order in range(2):
            parts.append((m, order, large if order == wide else amount - large))
    bf, f32 = jnp.bfloat16, jnp.float32
    grouped = [[] for _ in range(8)]
    for _, _, w in parts:
        grouped[0].append(((2, nz, 2, rc, w), bf))
        grouped[1].append(((nz, 2, rc, w), bf))
        grouped[2].append(((nz, rc, w), bf))
        grouped[3].append(((nz, rc, w), bf))
        grouped[4].append(((2, rc, w), bf))
        grouped[5].append(((2, rc, w), bf))
        grouped[6].append(((rc, w), bf))
        grouped[7].append(((rc, w), bf))
    total = sum(w for _, _, w in parts)
    chunks = 2
    buffers = sum(grouped, []) + [
        ((2, rows, total), f32),
        ((rows, total), f32),
        (stem_weight.shape, bf),
        (w_qkv.shape, bf),
        (w_out.shape, bf),
        ((2, grid_count * tok + TC, pin), bf),
        ((TC, pin), bf),
        ((2, tok, width), bf),
        ((2, tok, width), bf),
        ((2, tok, qd // 2), bf),
        ((2, tok, qd // 2), bf),
        ((2, tok, span), bf),
        ((span // 128, 4, tok, 256), bf),
        ((span // 128, 3, tok, 256), bf),
        ((span // 128, tok, 256), f32),
        ((span // 128, 3, tok, 256), bf),
        ((span // 128, tok, 256), bf),
        ((tok, width), f32),
        ((tok, 128), f32),
        ((tok, qd + span), f32),
        ((tok, qd + span), f32),
        ((tok, qd), bf),
        ((tok, qd), bf),
        ((tok, qd), bf),
        ((tok, qd), f32),
        ((tok, w_qkv.shape[1]), bf),
        ((2 * grid_count, nz * rows, tok), bf),
        ((2, nz * rows, grid_count * tok), bf),
        ((chunks, 2, nz // 2, rc, pin // chunks), bf),
        ((chunks, nz // 2, rc, pin // chunks), bf),
        ((chunks, rc, pin // chunks), bf),
        ((chunks, rc, pin // chunks), bf),
        ((1, width), f32),
        ((2 * grid_count - 1, 1, width), f32),
        ((1, width), f32),
        ((nz - 1, 1, width), f32),
        ((width, 128), f32),
    ]
    dma = pltpu.SemaphoreType.DMA
    halves, count, others = span // 128, len(parts), 2 * grid_count - 1
    semaphores = [dma((6,)), dma((6,)), dma((6,)), dma((count,)), dma((count,)), dma, dma, dma((3,)), dma((3,)), dma((3,)), dma((3,))]
    semaphores += [dma((halves, 3)), dma((halves, 4)), dma((halves, 3)), dma((halves, 3)), dma((count, 2)), dma((count, 2))]
    semaphores += [dma((count, 2)), dma((count, 2)), dma((others,)), dma((others,)), dma((others,)), dma((others,))]
    semaphores += [dma((nz - 1,)), dma((nz - 1,)), dma((chunks, 2)), dma((chunks, 2))]
    vmem = pl.BlockSpec(memory_space=pltpu.VMEM)
    hbm = pl.BlockSpec(memory_space=pl.ANY)
    shapes = [
        jax.ShapeDtypeStruct(shape, f32)
        for shape in ((2, rows, pin), (1, rows), (rows, w_qkv.shape[1]), (rows, qd))
    ]
    results = pl.pallas_call(
        partial(layer_kernel, (nz, parts)),
        out_shape=shapes,
        in_specs=[pl.BlockSpec(memory_space=pltpu.SMEM), hbm, hbm, hbm, vmem, hbm, hbm, vmem],
        out_specs=[vmem] * 4,
        scratch_shapes=[pltpu.VMEM(shape, kind) for shape, kind in buffers] + semaphores,
        compiler_params=pltpu.CompilerParams(collective_id=0, has_side_effects=True, vmem_limit_bytes=63000000),
    )(per_head_scale, tiles, grad_out, stem_weight, norm_gain, w_qkv, w_out, positions.reshape(-1, tok))
    return pl.pallas_call(unpack_kernel, out_shape=shapes, in_specs=[vmem] * 4, out_specs=[vmem] * 4)(*results)


def shards(patches, stem_weight, norm_gain, w_qkv, w_out, per_head_scale, positions, d_out):
    tiles = patches[0]
    grad_out = d_out[0]
    if fits_planes(grad_out.shape[1]):
        d_stem, d_gain, d_qkv, d_out_t = whole_layer(
            tiles, grad_out, stem_weight, norm_gain, w_qkv, w_out, per_head_scale, positions
        )
        return (d_stem.transpose(0, 2, 1), d_gain.reshape(-1), d_qkv, d_out_t.T)
    token_rows = tiles.shape[0]
    group_factor = QUERY_HEADS // KEY_VALUE_HEADS
    query_span_width = QUERY_HEADS * HEAD_SIZE
    key_span_width = KEY_VALUE_HEADS * HEAD_SIZE
    arrived = shifted(tiles[:TC], "grid", -1)
    below = jnp.concatenate([tiles[TC:], arrived], axis=0)
    stem = jnp.dot(tiles, stem_weight[0], preferred_element_type=jnp.float32)
    stem = stem + jnp.dot(below, stem_weight[1], preferred_element_type=jnp.float32)
    token_f = lax.optimization_barrier(stem.astype(jnp.bfloat16)).astype(jnp.float32)
    gain_f = norm_gain.astype(jnp.float32)
    normed = row_norm(token_f)
    hidden = (normed * gain_f).astype(jnp.bfloat16)
    query_key_value = jnp.dot(hidden, w_qkv, preferred_element_type=jnp.float32)
    query = query_key_value[:, :query_span_width].reshape(token_rows, QUERY_HEADS, HEAD_SIZE)
    key = query_key_value[:, query_span_width : query_span_width + key_span_width].reshape(
        token_rows, KEY_VALUE_HEADS, HEAD_SIZE
    )
    query_normalized = head_norm(query).astype(jnp.bfloat16)
    key_n = head_norm(key).astype(jnp.bfloat16).reshape(token_rows, key_span_width)
    value = query_key_value[:, query_span_width + key_span_width :].astype(jnp.bfloat16)
    attention_gradient = jnp.dot(grad_out, w_out.T, preferred_element_type=jnp.float32).astype(
        jnp.bfloat16
    )
    kv_own = jnp.concatenate([key_n, value], axis=1)
    blk_count = lax.axis_size("blk")
    own_index = lax.axis_index("blk")
    blocks = [kv_own]
    for offset in range(1, 4):
        blocks.append(passed_along(kv_own, "blk", offset))
    causal_window = jnp.concatenate(blocks, axis=0)
    key_pos = jnp.concatenate(
        [
            lax.dynamic_slice_in_dim(
                positions, (own_index - offset) % blk_count * token_rows, token_rows
            )
            for offset in range(4)
        ]
    )
    query_pos = lax.dynamic_slice_in_dim(positions, own_index * token_rows, token_rows)
    visible = (key_pos[None, :] <= query_pos[:, None])[None]
    every_key = causal_window.shape[0]
    query_cube = query_normalized.reshape(token_rows, KEY_VALUE_HEADS, group_factor, HEAD_SIZE)
    gradient_cube = attention_gradient.reshape(token_rows, KEY_VALUE_HEADS, group_factor, HEAD_SIZE)
    key_cube = causal_window[:, :key_span_width].reshape(every_key, KEY_VALUE_HEADS, HEAD_SIZE)
    value_cube = causal_window[:, key_span_width:].reshape(every_key, KEY_VALUE_HEADS, HEAD_SIZE)
    score_scales = per_head_scale.reshape(KEY_VALUE_HEADS, group_factor)
    prob_list = []
    low_list = []
    attn_list = []
    for query_head_group in range(KEY_VALUE_HEADS):
        scale_col = score_scales[query_head_group][:, None, None]
        attention_scores = (
            jnp.einsum(
                "trd,sd->rts",
                query_cube[:, query_head_group],
                key_cube[:, query_head_group],
                preferred_element_type=jnp.float32,
            )
            * scale_col
        )
        attention_scores = jnp.where(visible, attention_scores, -1e30)
        top = jnp.max(attention_scores, axis=-1, keepdims=True)
        weights = jnp.where(visible, jnp.exp(attention_scores - top), 0.0)
        probs = weights / jnp.sum(weights, axis=-1, keepdims=True)
        probability_narrow = probs.astype(jnp.bfloat16)
        prob_list.append(probs)
        low_list.append(probability_narrow)
        attn_list.append(
            jnp.einsum(
                "rts,sd->trd",
                probability_narrow,
                value_cube[:, query_head_group],
                preferred_element_type=jnp.float32,
            )
        )
    attention_output = (
        jnp.stack(attn_list, axis=1).reshape(token_rows, query_span_width).astype(jnp.bfloat16)
    )
    dquery_list = []
    dkey_list = []
    dvalue_list = []
    for query_head_group in range(KEY_VALUE_HEADS):
        scale_col = score_scales[query_head_group][:, None, None]
        grad_group = gradient_cube[:, query_head_group]
        softmax_delta = jnp.sum(
            grad_group.astype(jnp.float32) * attn_list[query_head_group], axis=-1
        )
        probability_gradient = jnp.einsum(
            "trd,sd->rts",
            grad_group,
            value_cube[:, query_head_group],
            preferred_element_type=jnp.float32,
        )
        score_gradient = (
            scale_col
            * prob_list[query_head_group]
            * (probability_gradient - softmax_delta.T[:, :, None])
        ).astype(jnp.bfloat16)
        dquery_list.append(
            jnp.einsum(
                "rts,sd->trd",
                score_gradient,
                key_cube[:, query_head_group],
                preferred_element_type=jnp.float32,
            )
        )
        dkey_list.append(
            jnp.einsum(
                "rts,trd->sd",
                score_gradient,
                query_cube[:, query_head_group],
                preferred_element_type=jnp.float32,
            )
        )
        dvalue_list.append(
            jnp.einsum(
                "rts,trd->sd",
                low_list[query_head_group],
                grad_group,
                preferred_element_type=jnp.float32,
            )
        )
    query_gradient = jnp.stack(dquery_list, axis=1).reshape(token_rows, QUERY_HEADS, HEAD_SIZE)
    dkey_all = jnp.stack(dkey_list, axis=1).reshape(every_key, key_span_width)
    dvalue_all = jnp.stack(dvalue_list, axis=1).reshape(every_key, key_span_width)
    partial_terms = jnp.concatenate([dkey_all, dvalue_all], axis=1)
    pieces = [partial_terms[offset * token_rows : (offset + 1) * token_rows] for offset in range(4)]
    carried_state = pieces[0]
    for offset in (1, 2, 3):
        carried_state = carried_state + passed_along(pieces[offset], "blk", -offset)
    pull_query = jax.vjp(head_norm, query)[1]
    gather_key = jax.vjp(head_norm, key)[1]
    dq_full = pull_query(query_gradient)[0].reshape(token_rows, query_span_width)
    key_gradient_whole = gather_key(
        carried_state[:, :key_span_width].reshape(token_rows, KEY_VALUE_HEADS, HEAD_SIZE)
    )[0].reshape(token_rows, key_span_width)
    d_qkv = jnp.concatenate(
        [dq_full, key_gradient_whole, carried_state[:, key_span_width:]], axis=1
    ).astype(jnp.bfloat16)
    d_hidden = jnp.dot(d_qkv, w_qkv.T, preferred_element_type=jnp.float32)
    gain_term = jnp.sum(d_hidden * normed, axis=0)
    pull_tokens = jax.vjp(row_norm, token_f)[1]
    d_tokens = (grad_out.astype(jnp.float32) + pull_tokens(d_hidden * gain_f)[0]).astype(
        jnp.bfloat16
    )
    stem_term = jnp.stack(
        [
            jnp.dot(tiles.T, d_tokens, preferred_element_type=jnp.float32),
            jnp.dot(below.T, d_tokens, preferred_element_type=jnp.float32),
        ]
    )
    qkv_term = jnp.dot(hidden.T, d_qkv, preferred_element_type=jnp.float32)
    out_term = jnp.dot(attention_output.T, grad_out, preferred_element_type=jnp.float32)
    d_stem_weight = lax.psum_scatter(stem_term, ("blk", "grid"), scatter_dimension=2, tiled=True)
    d_norm_gain = lax.psum_scatter(gain_term, ("blk", "grid"), scatter_dimension=0, tiled=True)
    d_w_qkv = lax.psum_scatter(qkv_term, ("blk", "grid"), scatter_dimension=0, tiled=True)
    d_w_out = lax.psum_scatter(out_term, ("blk", "grid"), scatter_dimension=1, tiled=True)
    return (d_stem_weight, d_norm_gain, d_w_qkv, d_w_out)


def solution(mesh):
    placed = (P("grid", "blk", None), P(), P(), P(), P(), P(), P(), P("grid", "blk", None))
    return jax.shard_map(
        shards,
        mesh=mesh,
        in_specs=placed,
        out_specs=(
            P(None, None, ("blk", "grid")),
            P(("blk", "grid")),
            P(("blk", "grid"), None),
            P(None, ("blk", "grid")),
        ),
        check_vma=False,
    )
```

```python
from functools import partial

import jax
import jax.numpy as jnp
from jax import lax
from jax.experimental import pallas as pl
from jax.experimental.pallas import tpu as pltpu
from jax.sharding import PartitionSpec as P

QUERY_HEADS = 12
KEY_VALUE_HEADS = 4
HEAD_SIZE = 64
TC = 16


def shifted(x, axis, by):
    peers = lax.axis_size(axis)
    pairs = [(i, i + by) for i in range(peers) if 0 <= i + by < peers]
    return lax.ppermute(x, axis, pairs)


def passed_along(x, axis, by):
    peers = lax.axis_size(axis)
    return lax.ppermute(x, axis, [(i, (i + by) % peers) for i in range(peers)])


def row_norm(values):
    return values * lax.rsqrt(jnp.mean(values * values, axis=-1, keepdims=True) + 1e-05)


def head_norm(values):
    return values * lax.rsqrt(jnp.mean(values * values, axis=-1, keepdims=True) + 1e-06)


def transposed_dot(a, b):
    return lax.dot_general(a, b, (((0,), (0,)), ((), ())), preferred_element_type=jnp.float32)


def rowwise_dot(a, b):
    return lax.dot_general(a, b, (((1,), (1,)), ((), ())), preferred_element_type=jnp.float32)


def plain_dot(a, b):
    return jnp.dot(a, b, preferred_element_type=jnp.float32)


def half_sums(x):
    low = lax.broadcasted_iota(jnp.int32, x.shape, 1) < HEAD_SIZE
    first = jnp.sum(jnp.where(low, x, 0.0), axis=1, keepdims=True)
    second = jnp.sum(jnp.where(low, 0.0, x), axis=1, keepdims=True)
    return jnp.where(low, first, second)


DIRECT_KEYS = 1
CHAINED = 2


def fits_planes(width):
    blocks, bands = lax.axis_size("blk"), lax.axis_size("grid")
    devices = blocks * bands
    return bands == 4 and blocks == 8 and width % devices == 0 and (width // devices) % 8 == 0


def chip_partner(bit, own_blk, own_grid):
    if bit == 0:
        mine = own_grid // 2
        return {"blk": own_blk, "grid": own_grid + (1 - 2 * mine) * 2}, mine
    step = 1 << (bit - 1)
    mine = own_blk // step % 2
    return {"blk": own_blk + (1 - 2 * mine) * step, "grid": own_grid}, mine


def layer_kernel(plan, *refs):
    nz, parts = plan
    (scale_ref, tiles_hbm, grad_hbm, stem_hbm, gain_ref, wqkv_hbm, wout_hbm, pos_ref) = refs[:8]
    (stem_out, gain_out, qkv_out, out_out) = refs[8:12]
    scratch = list(refs[12:])
    count = len(parts)
    nb = len(parts[0][1])
    first = [scratch.pop(0) for _ in range(count)]
    recv = [[scratch.pop(0) for _ in range(nb)] for _ in range(count)]
    send = [[None] + [scratch.pop(0) for _ in range(nb - 1)] for _ in range(count)]
    keep = [[scratch.pop(0) for _ in range(nb - 1)] for _ in range(count)]
    (final, final_recv, stem_w, wqkv, wout, image, halo_rows, grad_pair, hidden_pair, attn_pair, dq_pair, dkv_pair,
     kv, dkv_out, dkv_own, dkv_in, dkv_mid, dkv_side, normed_ref, inv_ref, qk_ref, heads_inv, qn, da, attn, dq, dqkv,
     tok_out, tok_all, stem_send, stem_got, stem_next, stem_last, gain_own, gain_got, gain_plane, gain_z, gain_col,
     load_sem, pair_send, pair_got, final_send, final_got, halo_send, halo_got, tile_send, tile_got, pass_send, pass_got,
     kv_send, kv_got, dkv_send, dkv_got, part_send, part_got, tok_send, tok_got, gain_send, gain_arrived,
     gain_z_send, gain_z_got, stem_sent, stem_arrived) = scratch
    tok, width = grad_pair.shape[1:]
    halo = halo_rows.shape[0]
    pin = image.shape[2]
    span = kv.shape[0] * HEAD_SIZE
    group = QUERY_HEADS // KEY_VALUE_HEADS
    own_blk = lax.axis_index("blk")
    own_grid = lax.axis_index("grid")
    blk_count = lax.axis_size("blk")
    grid_count = lax.axis_size("grid")
    core = own_grid % 2
    own_y = own_grid // 2
    own_x = own_blk % 2
    own_z = own_blk // 2
    z_low, z_high = own_z % 2, own_z // 2
    rows = width // (blk_count * grid_count)
    other_core = {"blk": own_blk, "grid": own_grid + 1 - 2 * core}
    above = {"blk": own_blk, "grid": (own_grid + grid_count - 1) % grid_count}
    plane = [(i, j) for i in range(2) for j in range(grid_count) if i + j > 0]

    def along(offset):
        return {"blk": (own_blk + offset + blk_count) % blk_count, "grid": own_grid}

    def beside(i, j):
        return {"blk": own_z * 2 + (own_x + i) % 2, "grid": (own_grid + j) % grid_count}

    def level(k):
        return {"blk": (own_z + k) % nz * 2 + own_x, "grid": own_grid}

    z_near = {"blk": own_blk + (1 - 2 * z_low) * 2, "grid": own_grid}
    z_far = {"blk": own_blk + (1 - 2 * z_high) * 4, "grid": own_grid}

    own_rows = pl.ds(pl.multiple_of(own_grid * tok, tok), tok)
    loads = [
        pltpu.make_async_copy(tiles_hbm, image.at[own_x, own_rows], load_sem.at[0]),
        pltpu.make_async_copy(stem_hbm.at[0], stem_w.at[0], load_sem.at[1]),
        pltpu.make_async_copy(stem_hbm.at[1], stem_w.at[1], load_sem.at[2]),
        pltpu.make_async_copy(wqkv_hbm, wqkv, load_sem.at[3]),
        pltpu.make_async_copy(grad_hbm, grad_pair.at[core], load_sem.at[4]),
        pltpu.make_async_copy(wout_hbm, wout, load_sem.at[5]),
    ]
    barrier = pltpu.get_barrier_semaphore()
    peers = [beside(i, j) for i, j in plane] + [level(k) for k in range(1, nz)] + [along(j) for j in (1, 2, 3, -1, -2, -3)]
    for peer in peers:
        pl.semaphore_signal(barrier, inc=1, device_id=peer, device_id_type=pl.DeviceIdType.MESH)
    for load in loads:
        load.start()
    image[:, grid_count * tok :] = jnp.zeros((2, halo, pin), image.dtype)

    def push(source, target, sems, got, device):
        copy = pltpu.make_async_remote_copy(
            src_ref=source, dst_ref=target, send_sem=sems, recv_sem=got, device_id=device, device_id_type=pl.DeviceIdType.MESH
        )
        copy.start()
        return copy

    def all_of(ref, sems, got):
        return pltpu.make_async_remote_copy(
            src_ref=ref, dst_ref=ref, send_sem=sems, recv_sem=got, device_id=other_core, device_id_type=pl.DeviceIdType.MESH
        )

    def pair(which, source, target):
        return push(source, target, pair_send.at[which], pair_got.at[which], other_core)

    def tiles_to(slot, i, j):
        mine = image.at[own_x, own_rows]
        return push(mine, mine, tile_send.at[slot], tile_got.at[slot], beside(i, j))

    loads[0].wait()
    pl.semaphore_wait(barrier, len(peers))
    halo_copy = push(image.at[own_x, pl.ds(pl.multiple_of(own_grid * tok, tok), halo)], halo_rows, halo_send, halo_got, above)
    tile_copies = [tiles_to(0, 0, 2), tiles_to(1, 1, 0)]
    tile_pair = pair(0, image.at[own_x, own_rows], image.at[own_x, own_rows])

    loads[1].wait()
    tiles = image[own_x, own_rows]
    stem = plain_dot(tiles, stem_w[0])
    loads[2].wait()
    halo_copy.wait()

    @pl.when(own_grid == grid_count - 1)
    def _():
        halo_rows[...] = jnp.zeros(halo_rows.shape, halo_rows.dtype)

    below = jnp.concatenate([tiles[halo:], halo_rows[...]], axis=0)
    stem = stem + plain_dot(below, stem_w[1])
    token_f = stem.astype(jnp.bfloat16).astype(jnp.float32)
    inv = lax.rsqrt(jnp.sum(token_f * token_f, axis=1, keepdims=True) / width + 1e-05)
    normed = token_f * inv
    normed_ref[...] = normed
    inv_ref[...] = jnp.broadcast_to(inv, inv_ref.shape)
    gain_f = gain_ref[...].astype(jnp.float32).reshape(1, width)
    hidden = (normed * gain_f).astype(jnp.bfloat16)
    hidden_pair[core] = hidden
    loads[3].wait()
    key_start = QUERY_HEADS * HEAD_SIZE

    def normalize(x):
        scale = lax.rsqrt(half_sums(x * x) / HEAD_SIZE + 1e-06)
        return scale, (x * scale).astype(jnp.bfloat16)

    keys = plain_dot(hidden, wqkv[:, key_start:])
    def kv_push(g, source, slot, which, device):
        return push(kv.at[g, source], kv.at[g, slot], kv_send.at[which], kv_got.at[g, slot], device)

    def kv_copy(g, slot, which):
        return pltpu.make_async_remote_copy(
            src_ref=kv.at[g, 0], dst_ref=kv.at[g, slot], send_sem=kv_send.at[which], recv_sem=kv_got.at[g, slot],
            device_id=along(2), device_id_type=pl.DeviceIdType.MESH,
        )

    for u in range(span // 128):
        at = u * 128
        heads_inv[:, key_start + at : key_start + at + 128], key_n = normalize(keys[:, at : at + 128])
        value = keys[:, span + at : span + at + 128].astype(jnp.bfloat16)
        for e in range(2):
            g, lanes = 2 * u + e, slice(e * HEAD_SIZE, (e + 1) * HEAD_SIZE)
            kv[g, 0] = jnp.concatenate([key_n[:, lanes], value[:, lanes]], axis=1)
            kv_push(g, 0, 2, 0, along(2))
            if g < DIRECT_KEYS:
                kv_push(g, 0, 1 + 2 * own_x, 1, along(1 + 2 * own_x))
            else:

                @pl.when(own_x == 0)
                def _():
                    kv_push(g, 0, 1, 1, along(1))

    qk_ref[:, key_start:] = keys[:, :span]
    loads[4].wait()
    grad_copy = pair(1, grad_pair.at[core], grad_pair.at[core])
    hidden_copy = pair(2, hidden_pair.at[core], hidden_pair.at[core])
    queries = plain_dot(hidden, wqkv[:, :key_start])
    qk_ref[:, :key_start] = queries
    for at in range(0, key_start, 128):
        heads_inv[:, at : at + 128], qn[:, at : at + 128] = normalize(queries[:, at : at + 128])
    loads[5].wait()
    grad_own = grad_pair[core]
    da[...] = rowwise_dot(grad_own, wout[...]).astype(jnp.bfloat16)

    query_pos = pos_ref[pl.ds(own_blk, 1), :]
    seen = []
    for j in range(4):
        key_pos = pos_ref[pl.ds((own_blk + blk_count - j) % blk_count, 1), :]
        column = jnp.broadcast_to(key_pos, (tok, tok)).T
        seen.append(column <= query_pos)
    visible = jnp.concatenate([jnp.where(x, 1.0, 0.0) for x in seen], axis=0) > 0.5
    def pass_up(g):
        kv_copy(g, 1, 3).wait_recv()

        @pl.when(own_x == 0)
        def _():
            kv_push(g, 1, 3, 3, along(2))

    for g in range(KEY_VALUE_HEADS):
        kv_copy(g, 2, 0).wait_recv()
        kv_push(g, 2, 3 - 2 * own_x, 2, beside(1, 0))
        if g > DIRECT_KEYS:
            pass_up(g - 1)

    def dkv_push(source, g, slot, which, device):
        return push(source, dkv_in.at[g, slot], dkv_send.at[which], dkv_got.at[g, slot], device)

    def dkv_copy_of(g, slot, which):
        return pltpu.make_async_remote_copy(
            src_ref=dkv_out.at[g, 0], dst_ref=dkv_in.at[g, slot], send_sem=dkv_send.at[which], recv_sem=dkv_got.at[g, slot],
            device_id=along(2), device_id_type=pl.DeviceIdType.MESH,
        )

    def give(g):
        if g < CHAINED:
            dkv_push(dkv_out.at[g, 2 - 2 * own_x], g, 3 * own_x, 0, along(own_x - 2))
        else:
            dkv_push(dkv_out.at[g, 2 * own_x], g, 1, 1, beside(1, 0))
            dkv_push(dkv_out.at[g, 2 - 2 * own_x], g, 0, 0, along(2 * own_x - 3))

    def sideways(g):
        @pl.when(own_x == 0)
        def _():
            dkv_copy_of(g, 0, 0).wait_recv()
            dkv_side[g] = (dkv_out[g, 0].astype(jnp.float32) + dkv_in[g, 0].astype(jnp.float32)).astype(jnp.bfloat16)

        @pl.when(own_x == 1)
        def _():
            dkv_side[g] = dkv_out[g, 2]

        dkv_push(dkv_side.at[g], g, 1, 1, beside(1, 0))

    def combine(g):
        dkv_copy_of(g, 1, 1).wait_recv()
        dkv_mid[g] = (dkv_out[g, 1].astype(jnp.float32) + dkv_in[g, 1].astype(jnp.float32)).astype(jnp.bfloat16)
        dkv_push(dkv_mid.at[g], g, 2, 2, along(-2))

    for g in range(KEY_VALUE_HEADS):
        if g <= DIRECT_KEYS - 1 or g == KEY_VALUE_HEADS:
            kv_copy(g, 1, 3).wait_recv()
        kv_copy(g, 3, 2).wait_recv()
        if g == 2:
            tile_copies[1].wait()
            near = image.at[1 - own_x, own_rows]
            tile_copies.append(push(near, near, tile_send.at[2], tile_got.at[2], beside(0, 2)))
        keys_g = kv[g, :, :, :HEAD_SIZE].reshape(4 * tok, HEAD_SIZE)
        values_g = kv[g, :, :, HEAD_SIZE:].reshape(4 * tok, HEAD_SIZE)
        heads = [slice((g * group + i) * HEAD_SIZE, (g * group + i + 1) * HEAD_SIZE) for i in range(group)]
        queries_g = jnp.concatenate([qn[:, h] for h in heads], axis=0)
        grads_g = jnp.concatenate([da[:, h] for h in heads], axis=0)
        scores = rowwise_dot(keys_g, queries_g)
        dprobs = rowwise_dot(values_g, grads_g)
        probs, low = [], []
        for i in range(group):
            s = jnp.where(visible, scores[:, i * tok : (i + 1) * tok] * scale_ref[g * group + i], -1e30)
            weights = jnp.where(visible, jnp.exp(s - jnp.max(s, axis=0, keepdims=True)), 0.0)
            p = weights * (1.0 / jnp.sum(weights, axis=0, keepdims=True))
            probs.append(p)
            low.append(p.astype(jnp.bfloat16))
        low_g = jnp.concatenate(low, axis=1)
        attn_t = transposed_dot(values_g, low_g)
        delta = jnp.sum(grads_g.astype(jnp.float32).T * attn_t, axis=0, keepdims=True)
        ds = []
        for i in range(group):
            cols = slice(i * tok, (i + 1) * tok)
            ds.append((scale_ref[g * group + i] * probs[i] * (dprobs[:, cols] - delta[:, cols])).astype(jnp.bfloat16))
        ds_g = jnp.concatenate(ds, axis=1)
        dq_g = transposed_dot(keys_g, ds_g).T
        attn_g = attn_t.T
        for i in range(group):
            attn[:, heads[i]] = attn_g[i * tok : (i + 1) * tok].astype(jnp.bfloat16)
            dq[:, heads[i]] = dq_g[i * tok : (i + 1) * tok]
        dkeys = plain_dot(ds_g, queries_g).reshape(4, tok, HEAD_SIZE)
        dvalues = plain_dot(low_g, grads_g).reshape(4, tok, HEAD_SIZE)
        dkv_own[g] = jnp.concatenate([dkeys[0], dvalues[0]], axis=1)
        for j in (1, 2, 3):
            dkv_out[g, j - 1] = jnp.concatenate([dkeys[j], dvalues[j]], axis=1).astype(jnp.bfloat16)
        give(g)
        if g == 0:
            pass_up(KEY_VALUE_HEADS - 1)
        if 0 <= g - 1 < CHAINED:
            sideways(g - 1)
        if g >= 2:
            combine(g - 2)
    half = key_start // 2

    def half_of(start, amount, which):
        return pl.ds(pl.multiple_of(start + which * amount, 128), amount)

    attn_copy = pair(3, attn.at[:, half_of(0, half, 1 - core)], attn_pair.at[core])
    attn_pair[core] = attn[:, half_of(0, half, core)]

    def pull(at, g):
        scale = heads_inv[:, at : at + 128]
        x = qk_ref[:, at : at + 128] * scale
        return (scale * (g - x * (half_sums(g * x) / HEAD_SIZE))).astype(jnp.bfloat16)

    for at in range(0, key_start, 128):
        dqkv[:, at : at + 128] = pull(at, dq[:, at : at + 128])
    dq_copy = pair(4, dqkv.at[:, half_of(0, half, 1 - core)], dq_pair.at[core])
    dq_pair[core] = dqkv[:, half_of(0, half, core)]

    copies = [None] * count
    steps = [0] * count
    starts = [sum(w for _, _, w in parts[:p]) for p in range(count)]

    def transfer(p, source):
        partner = chip_partner(parts[p][1][steps[p]], own_blk, own_grid)[0]
        copies[p] = push(source, recv[p][steps[p]], part_send.at[steps[p]], part_got.at[p, steps[p]], partner)

    def begin(members, left, right):
        product = transposed_dot(left.reshape(2 * tok, width), right).astype(jnp.bfloat16)
        at = 0
        for p in members:
            order, w = parts[p][1:]
            first[p][...] = product[:, at : at + w].reshape(first[p].shape)
            at += w
            if order[0] < 2:
                launch(p)

    def launch(p):
        mine = chip_partner(parts[p][1][0], own_blk, own_grid)[1]
        transfer(p, first[p].at[:, 1 - mine])

    def advance(p):
        step, order = steps[p], parts[p][1]
        copies[p].wait_recv()
        held = recv[p][step]
        mine = chip_partner(order[step], own_blk, own_grid)[1]
        left_over = [b for b in range(nb) if b not in order[:step]]
        inner = first[p].shape[2]

        def total(i):
            if step == 0:
                return first[p][i // inner, mine, i % inner].astype(jnp.float32) + held[i // inner, i % inner].astype(jnp.float32)
            return keep[p][step - 1][i] + held[i].astype(jnp.float32)

        steps[p] = step + 1
        if step == nb - 1:
            value = total(0)
            cols = slice(starts[p], starts[p] + parts[p][2])
            final[0, :, cols] = value[:rows]
            final[1, :, cols] = value[rows:]
            push(final.at[1 - core, :, cols], final_recv.at[:, cols], final_send, final_got, other_core)
            return
        left_over.remove(order[step])
        place_next = 1 << left_over.index(order[step + 1])
        mine_next = chip_partner(order[step + 1], own_blk, own_grid)[1]
        amount = 1 << (nb - 2 - step)
        for r in range(amount):
            away = r // place_next * (2 * place_next) + (1 - mine_next) * place_next + r % place_next
            send[p][step + 1][r] = total(away).astype(jnp.bfloat16)
        transfer(p, send[p][step + 1])
        for r in range(amount):
            here = r // place_next * (2 * place_next) + mine_next * place_next + r % place_next
            keep[p][step][r] = total(here)

    def advance_all(members):
        for p in members:
            advance(p)

    of_out, of_query, of_key = [[p for p in range(count) if parts[p][0] == m] for m in range(3)]
    attn_copy.wait()
    grad_copy.wait()
    begin(of_out, grad_pair[...], attn_pair[...].reshape(2 * tok, half))
    for g in range(KEY_VALUE_HEADS - 2, KEY_VALUE_HEADS):
        combine(g)
    launch(of_out[2])
    for slot, (i, j) in enumerate(((0, 2), (1, 0), (1, 2))):
        if slot != 1:
            tile_copies[slot].wait()
        where = image.at[(own_x + i) % 2, pl.ds(pl.multiple_of((own_grid + j) % grid_count * tok, tok), tok)]
        push(where, where, pass_send, pass_got, other_core)

    advance_all(of_out[:2])
    for g in range(KEY_VALUE_HEADS):
        if g < CHAINED:

            @pl.when(own_x == 0)
            def _():
                dkv_copy_of(g, 3, 0).wait_recv()
                dkv_own[g] += dkv_in[g, 3].astype(jnp.float32)

        else:
            dkv_copy_of(g, 0, 0).wait_recv()
        dkv_copy_of(g, 2, 2).wait_recv()
    for u in range(span // 128):
        sums = []
        for g in (2 * u, 2 * u + 1):
            total_kv = dkv_own[g] + dkv_in[g, 2].astype(jnp.float32)
            if g >= CHAINED:
                total_kv = total_kv + dkv_in[g, 0].astype(jnp.float32)
            sums.append(total_kv)
        at = key_start + u * 128
        dqkv[:, at : at + 128] = pull(at, jnp.concatenate([x[:, :HEAD_SIZE] for x in sums], axis=1))
        d_value = jnp.concatenate([x[:, HEAD_SIZE:] for x in sums], axis=1)
        dqkv[:, at + span : at + span + 128] = d_value.astype(jnp.bfloat16)
    dkv_copy = pair(5, dqkv.at[:, half_of(key_start, span, 1 - core)], dkv_pair.at[core])
    dkv_pair[core] = dqkv[:, half_of(key_start, span, core)]
    d_hidden = rowwise_dot(dqkv[...], wqkv[...])
    normed = normed_ref[...]
    flow = d_hidden * gain_f
    inner_mean = jnp.sum(flow * normed, axis=1, keepdims=True) / width
    d_tokens = grad_pair[core].astype(jnp.float32) + inv_ref[:, :1] * (flow - normed * inner_mean)
    turned = d_tokens.T
    for c in range(4 * 2):
        pieces = [turned[(r * 8 + c) * rows : (r * 8 + c + 1) * rows] for r in range(nz)]
        tok_out[c] = jnp.concatenate(pieces, axis=0).astype(jnp.bfloat16)
    own_lanes = pl.ds(pl.multiple_of(own_grid * tok, tok), tok)
    gain_own[...] = jnp.sum(d_hidden * normed, axis=0, keepdims=True)
    for i, j in plane:
        to_grid = (own_grid + j) % grid_count
        goal = (own_x + i) % 2 * grid_count + to_grid
        push(tok_out.at[goal], tok_all.at[own_x, :, own_lanes], tok_send, tok_got, beside(i, j))
    for slot, (i, j) in enumerate(plane):
        push(gain_own, gain_got.at[slot], gain_send, gain_arrived, beside(i, j))
    tok_all[own_x, :, own_lanes] = tok_out[own_x * grid_count + own_grid]

    dq_copy.wait()
    hidden_copy.wait()
    begin(of_query, hidden_pair[...], dq_pair[...].reshape(2 * tok, half))

    advance_all(of_out[:2])
    dkv_copy.wait()
    begin(of_key, hidden_pair[...], dkv_pair[...].reshape(2 * tok, span))
    advance(of_out[2])
    tile_pair.wait()
    all_of(image.at[0, : 3 * tok], pass_send, pass_got).wait()
    all_of(tok_out.at[: len(plane)], tok_send, tok_got).wait()
    chunks = stem_send.shape[0]
    step = pin // chunks
    stem_copies = []
    for h in range(chunks):
        cols = slice(h * step, (h + 1) * step)
        straight = plain_dot(tok_all[0], image[0, : grid_count * tok, cols]) + plain_dot(tok_all[1], image[1, : grid_count * tok, cols])
        lower = plain_dot(tok_all[0], image[0, halo:, cols]) + plain_dot(tok_all[1], image[1, halo:, cols])
        for r in range(nz):
            both = jnp.concatenate([straight[r * rows : (r + 1) * rows], lower[r * rows : (r + 1) * rows]], axis=0)
            stem_send[h, r % 2, r // 2] = both.astype(jnp.bfloat16)
        stem_copies.append(push(stem_send.at[h, 1 - z_low], stem_got.at[h], stem_sent.at[0], stem_arrived.at[h, 0], z_near))

    def stem_near(h, k):
        return stem_send[h, z_low, k].astype(jnp.float32) + stem_got[h, k].astype(jnp.float32)

    def stem_beyond(h):
        stem_copies[h].wait_recv()
        stem_next[h] = stem_near(h, 1 - z_high).astype(jnp.bfloat16)
        stem_copies[h] = push(stem_next.at[h], stem_last.at[h], stem_sent.at[1], stem_arrived.at[h, 1], z_far)

    all_of(gain_got, gain_send, gain_arrived).wait()
    gain_sum = gain_own[...]
    for slot in range(len(plane)):
        gain_sum = gain_sum + gain_got[slot]
    gain_plane[...] = gain_sum
    for k in range(1, nz):
        push(gain_plane, gain_z.at[k - 1], gain_z_send, gain_z_got, level(k))
    advance_all(of_query + of_out + of_key)
    for h in range(chunks):
        stem_beyond(h)
    advance_all(of_query + of_key + of_out[2:])
    advance_all(of_query + of_out[:2] + of_key + of_out[2:])
    advance_all(of_query)
    all_of(gain_z, gain_z_send, gain_z_got).wait()
    gain_sum = gain_plane[...]
    for k in range(nz - 1):
        gain_sum = gain_sum + gain_z[k]
    gain_col[...] = jnp.broadcast_to(gain_sum, (128, width)).T
    own_gain = gain_col[pl.ds(pl.multiple_of((own_blk * grid_count + own_grid) * rows, 8), rows), :]
    square = jnp.concatenate([own_gain, jnp.zeros((128 - rows, 128), jnp.float32)], axis=0).T
    gain_out[...] = square[:1, :rows]
    advance_all(of_key)
    for h in range(chunks):
        stem_copies[h].wait_recv()
        total = stem_near(h, z_high) + stem_last[h].astype(jnp.float32)
        cols = slice(h * step, (h + 1) * step)
        stem_out[0, :, cols] = total[:rows]
        stem_out[1, :, cols] = total[rows:]
    all_of(final.at[0], final_send, final_got).wait()
    all_of(kv.at[:, 0], kv_send.at[0], final_got).wait_send()
    all_of(kv.at[:, 0], kv_send.at[2], final_got).wait_send()

    @pl.when(own_x == 0)
    def _():
        all_of(kv.at[:, 0], kv_send.at[1], final_got).wait_send()
        all_of(kv.at[DIRECT_KEYS:, 0], kv_send.at[3], final_got).wait_send()

    @pl.when(own_x == 1)
    def _():
        all_of(kv.at[:DIRECT_KEYS, 0], kv_send.at[1], final_got).wait_send()

    for which in range(3):
        all_of(dkv_mid, dkv_send.at[which], final_got).wait_send()
    for step in range(nb):
        amount = count * (1 << (nb - 1 - step)) * 2 * rows * 128 // pin
        all_of(image.at[0, :amount], part_send.at[step], final_got).wait_send()
    all_of(stem_got, stem_sent.at[0], final_got).wait_send()
    all_of(stem_last, stem_sent.at[1], final_got).wait_send()
    for source, which in ((final.at[core], core), (final_recv, 1 - core)):
        out_out[:, half_of(0, half, which)] = source[:, :half]
        qkv_out[:, half_of(0, half, which)] = source[:, half : 2 * half]
        qkv_out[:, half_of(key_start, span, which)] = source[:, 2 * half :]


def unpack_kernel(*refs):
    half = len(refs) // 2
    for source, target in zip(refs[:half], refs[half:]):
        target[...] = source[...]


def whole_layer(tiles, grad_out, stem_weight, norm_gain, w_qkv, w_out, per_head_scale, positions):
    blk_count, grid_count = lax.axis_size("blk"), lax.axis_size("grid")
    nz = blk_count // 2
    tok, width = grad_out.shape
    pin = tiles.shape[1]
    qd, span = QUERY_HEADS * HEAD_SIZE, KEY_VALUE_HEADS * HEAD_SIZE
    rows = width // (blk_count * grid_count)
    rc = 2 * rows
    parts = []
    for m, orders in enumerate((((1, 0, 2, 3), (0, 1, 2, 3), (2, 1, 0, 3)), ((1, 0, 2, 3), (0, 1, 2, 3), (0, 1, 2, 3)), ((1, 0, 2, 3), (0, 1, 2, 3)))):
        parts += [(m, order, 128) for order in orders]
    nb = 4
    bf, f32 = jnp.bfloat16, jnp.float32
    firsts, recvs, sends, keeps = [], [], [], []
    for _, order, w in parts:
        inner = 1 << order[0]
        outer = (1 << nb) // (2 * inner)
        firsts.append(((outer, 2, inner, rc, w), bf))
        recvs.append(((outer, inner, rc, w), bf))
        for step in range(1, nb):
            shape = (1 << (nb - 1 - step), rc, w)
            recvs.append((shape, bf))
            sends.append((shape, bf))
            keeps.append((shape, f32))
    total = sum(w for _, _, w in parts)
    chunks, heads = 4, KEY_VALUE_HEADS
    buffers = firsts + recvs + sends + keeps + [
        ((2, rows, total), f32),
        ((rows, total), f32),
        (stem_weight.shape, bf),
        (w_qkv.shape, bf),
        (w_out.shape, bf),
        ((2, grid_count * tok + TC, pin), bf),
        ((TC, pin), bf),
        ((2, tok, width), bf),
        ((2, tok, width), bf),
        ((2, tok, qd // 2), bf),
        ((2, tok, qd // 2), bf),
        ((2, tok, span), bf),
        ((heads, 4, tok, 2 * HEAD_SIZE), bf),
        ((heads, 3, tok, 2 * HEAD_SIZE), bf),
        ((heads, tok, 2 * HEAD_SIZE), f32),
        ((heads, 4, tok, 2 * HEAD_SIZE), bf),
        ((heads, tok, 2 * HEAD_SIZE), bf),
        ((heads, tok, 2 * HEAD_SIZE), bf),
        ((tok, width), f32),
        ((tok, 128), f32),
        ((tok, qd + span), f32),
        ((tok, qd + span), f32),
        ((tok, qd), bf),
        ((tok, qd), bf),
        ((tok, qd), bf),
        ((tok, qd), f32),
        ((tok, w_qkv.shape[1]), bf),
        ((2 * grid_count, nz * rows, tok), bf),
        ((2, nz * rows, grid_count * tok), bf),
        ((chunks, 2, nz // 2, rc, pin // chunks), bf),
        ((chunks, nz // 2, rc, pin // chunks), bf),
        ((chunks, rc, pin // chunks), bf),
        ((chunks, rc, pin // chunks), bf),
        ((1, width), f32),
        ((2 * grid_count - 1, 1, width), f32),
        ((1, width), f32),
        ((nz - 1, 1, width), f32),
        ((width, 128), f32),
    ]
    dma = pltpu.SemaphoreType.DMA
    count = len(parts)
    semaphores = [dma((6,)), dma((6,)), dma((6,)), dma, dma, dma, dma, dma((3,)), dma((3,)), dma, dma]
    semaphores += [dma((4,)), dma((heads, 4)), dma((3,)), dma((heads, 4)), dma((nb,)), dma((count, nb))]
    semaphores += [dma] * 6 + [dma((2,)), dma((chunks, 2))]
    vmem = pl.BlockSpec(memory_space=pltpu.VMEM)
    hbm = pl.BlockSpec(memory_space=pl.ANY)
    shapes = [
        jax.ShapeDtypeStruct(shape, f32)
        for shape in ((2, rows, pin), (1, rows), (rows, w_qkv.shape[1]), (rows, qd))
    ]
    inputs = (per_head_scale, tiles, grad_out, stem_weight, norm_gain, w_qkv, w_out, positions.reshape(-1, tok))
    results = pl.pallas_call(
        partial(layer_kernel, (nz, parts)),
        out_shape=shapes,
        in_specs=[pl.BlockSpec(memory_space=pltpu.SMEM), hbm, hbm, hbm, vmem, hbm, hbm, vmem],
        out_specs=[vmem] * 4,
        scratch_shapes=[pltpu.VMEM(shape, kind) for shape, kind in buffers] + semaphores,
        compiler_params=pltpu.CompilerParams(collective_id=0, has_side_effects=True, vmem_limit_bytes=56000000),
    )(*[pltpu.with_memory_space_constraint(value, pltpu.HBM) for value in inputs])
    return pl.pallas_call(
        unpack_kernel,
        out_shape=shapes,
        in_specs=[vmem] * 4,
        out_specs=[vmem] * 4,
        compiler_params=pltpu.CompilerParams(vmem_limit_bytes=4000000),
    )(*results)


def shards(patches, stem_weight, norm_gain, w_qkv, w_out, per_head_scale, positions, d_out):
    tiles = patches[0]
    grad_out = d_out[0]
    if fits_planes(grad_out.shape[1]):
        d_stem, d_gain, d_qkv, d_out_t = whole_layer(
            tiles, grad_out, stem_weight, norm_gain, w_qkv, w_out, per_head_scale, positions
        )
        return (d_stem.transpose(0, 2, 1), d_gain.reshape(-1), d_qkv, d_out_t.T)
    token_rows = tiles.shape[0]
    group_factor = QUERY_HEADS // KEY_VALUE_HEADS
    query_span_width = QUERY_HEADS * HEAD_SIZE
    key_span_width = KEY_VALUE_HEADS * HEAD_SIZE
    arrived = shifted(tiles[:TC], "grid", -1)
    below = jnp.concatenate([tiles[TC:], arrived], axis=0)
    stem = jnp.dot(tiles, stem_weight[0], preferred_element_type=jnp.float32)
    stem = stem + jnp.dot(below, stem_weight[1], preferred_element_type=jnp.float32)
    token_f = lax.optimization_barrier(stem.astype(jnp.bfloat16)).astype(jnp.float32)
    gain_f = norm_gain.astype(jnp.float32)
    normed = row_norm(token_f)
    hidden = (normed * gain_f).astype(jnp.bfloat16)
    query_key_value = jnp.dot(hidden, w_qkv, preferred_element_type=jnp.float32)
    query = query_key_value[:, :query_span_width].reshape(token_rows, QUERY_HEADS, HEAD_SIZE)
    key = query_key_value[:, query_span_width : query_span_width + key_span_width].reshape(
        token_rows, KEY_VALUE_HEADS, HEAD_SIZE
    )
    query_normalized = head_norm(query).astype(jnp.bfloat16)
    key_n = head_norm(key).astype(jnp.bfloat16).reshape(token_rows, key_span_width)
    value = query_key_value[:, query_span_width + key_span_width :].astype(jnp.bfloat16)
    attention_gradient = jnp.dot(grad_out, w_out.T, preferred_element_type=jnp.float32).astype(
        jnp.bfloat16
    )
    kv_own = jnp.concatenate([key_n, value], axis=1)
    blk_count = lax.axis_size("blk")
    own_index = lax.axis_index("blk")
    blocks = [kv_own]
    for offset in range(1, 4):
        blocks.append(passed_along(kv_own, "blk", offset))
    causal_window = jnp.concatenate(blocks, axis=0)
    key_pos = jnp.concatenate(
        [
            lax.dynamic_slice_in_dim(
                positions, (own_index - offset) % blk_count * token_rows, token_rows
            )
            for offset in range(4)
        ]
    )
    query_pos = lax.dynamic_slice_in_dim(positions, own_index * token_rows, token_rows)
    visible = (key_pos[None, :] <= query_pos[:, None])[None]
    every_key = causal_window.shape[0]
    query_cube = query_normalized.reshape(token_rows, KEY_VALUE_HEADS, group_factor, HEAD_SIZE)
    gradient_cube = attention_gradient.reshape(token_rows, KEY_VALUE_HEADS, group_factor, HEAD_SIZE)
    key_cube = causal_window[:, :key_span_width].reshape(every_key, KEY_VALUE_HEADS, HEAD_SIZE)
    value_cube = causal_window[:, key_span_width:].reshape(every_key, KEY_VALUE_HEADS, HEAD_SIZE)
    score_scales = per_head_scale.reshape(KEY_VALUE_HEADS, group_factor)
    prob_list = []
    low_list = []
    attn_list = []
    for query_head_group in range(KEY_VALUE_HEADS):
        scale_col = score_scales[query_head_group][:, None, None]
        attention_scores = (
            jnp.einsum(
                "trd,sd->rts",
                query_cube[:, query_head_group],
                key_cube[:, query_head_group],
                preferred_element_type=jnp.float32,
            )
            * scale_col
        )
        attention_scores = jnp.where(visible, attention_scores, -1e30)
        top = jnp.max(attention_scores, axis=-1, keepdims=True)
        weights = jnp.where(visible, jnp.exp(attention_scores - top), 0.0)
        probs = weights / jnp.sum(weights, axis=-1, keepdims=True)
        probability_narrow = probs.astype(jnp.bfloat16)
        prob_list.append(probs)
        low_list.append(probability_narrow)
        attn_list.append(
            jnp.einsum(
                "rts,sd->trd",
                probability_narrow,
                value_cube[:, query_head_group],
                preferred_element_type=jnp.float32,
            )
        )
    attention_output = (
        jnp.stack(attn_list, axis=1).reshape(token_rows, query_span_width).astype(jnp.bfloat16)
    )
    dquery_list = []
    dkey_list = []
    dvalue_list = []
    for query_head_group in range(KEY_VALUE_HEADS):
        scale_col = score_scales[query_head_group][:, None, None]
        grad_group = gradient_cube[:, query_head_group]
        softmax_delta = jnp.sum(
            grad_group.astype(jnp.float32) * attn_list[query_head_group], axis=-1
        )
        probability_gradient = jnp.einsum(
            "trd,sd->rts",
            grad_group,
            value_cube[:, query_head_group],
            preferred_element_type=jnp.float32,
        )
        score_gradient = (
            scale_col
            * prob_list[query_head_group]
            * (probability_gradient - softmax_delta.T[:, :, None])
        ).astype(jnp.bfloat16)
        dquery_list.append(
            jnp.einsum(
                "rts,sd->trd",
                score_gradient,
                key_cube[:, query_head_group],
                preferred_element_type=jnp.float32,
            )
        )
        dkey_list.append(
            jnp.einsum(
                "rts,trd->sd",
                score_gradient,
                query_cube[:, query_head_group],
                preferred_element_type=jnp.float32,
            )
        )
        dvalue_list.append(
            jnp.einsum(
                "rts,trd->sd",
                low_list[query_head_group],
                grad_group,
                preferred_element_type=jnp.float32,
            )
        )
    query_gradient = jnp.stack(dquery_list, axis=1).reshape(token_rows, QUERY_HEADS, HEAD_SIZE)
    dkey_all = jnp.stack(dkey_list, axis=1).reshape(every_key, key_span_width)
    dvalue_all = jnp.stack(dvalue_list, axis=1).reshape(every_key, key_span_width)
    partial_terms = jnp.concatenate([dkey_all, dvalue_all], axis=1)
    pieces = [partial_terms[offset * token_rows : (offset + 1) * token_rows] for offset in range(4)]
    carried_state = pieces[0]
    for offset in (1, 2, 3):
        carried_state = carried_state + passed_along(pieces[offset], "blk", -offset)
    pull_query = jax.vjp(head_norm, query)[1]
    gather_key = jax.vjp(head_norm, key)[1]
    dq_full = pull_query(query_gradient)[0].reshape(token_rows, query_span_width)
    key_gradient_whole = gather_key(
        carried_state[:, :key_span_width].reshape(token_rows, KEY_VALUE_HEADS, HEAD_SIZE)
    )[0].reshape(token_rows, key_span_width)
    d_qkv = jnp.concatenate(
        [dq_full, key_gradient_whole, carried_state[:, key_span_width:]], axis=1
    ).astype(jnp.bfloat16)
    d_hidden = jnp.dot(d_qkv, w_qkv.T, preferred_element_type=jnp.float32)
    gain_term = jnp.sum(d_hidden * normed, axis=0)
    pull_tokens = jax.vjp(row_norm, token_f)[1]
    d_tokens = (grad_out.astype(jnp.float32) + pull_tokens(d_hidden * gain_f)[0]).astype(
        jnp.bfloat16
    )
    stem_term = jnp.stack(
        [
            jnp.dot(tiles.T, d_tokens, preferred_element_type=jnp.float32),
            jnp.dot(below.T, d_tokens, preferred_element_type=jnp.float32),
        ]
    )
    qkv_term = jnp.dot(hidden.T, d_qkv, preferred_element_type=jnp.float32)
    out_term = jnp.dot(attention_output.T, grad_out, preferred_element_type=jnp.float32)
    d_stem_weight = lax.psum_scatter(stem_term, ("blk", "grid"), scatter_dimension=2, tiled=True)
    d_norm_gain = lax.psum_scatter(gain_term, ("blk", "grid"), scatter_dimension=0, tiled=True)
    d_w_qkv = lax.psum_scatter(qkv_term, ("blk", "grid"), scatter_dimension=0, tiled=True)
    d_w_out = lax.psum_scatter(out_term, ("blk", "grid"), scatter_dimension=1, tiled=True)
    return (d_stem_weight, d_norm_gain, d_w_qkv, d_w_out)


def solution(mesh):
    placed = (P("grid", "blk", None), P(), P(), P(), P(), P(), P(), P("grid", "blk", None))
    return jax.shard_map(
        shards,
        mesh=mesh,
        in_specs=placed,
        out_specs=(
            P(None, None, ("blk", "grid")),
            P(("blk", "grid")),
            P(("blk", "grid"), None),
            P(None, ("blk", "grid")),
        ),
        check_vma=False,
    )
```

```python
from functools import partial

import jax
import jax.numpy as jnp
from jax import lax
from jax.experimental import pallas as pl
from jax.experimental.pallas import tpu as pltpu
from jax.sharding import PartitionSpec as P

QUERY_HEADS = 12
KEY_VALUE_HEADS = 4
HEAD_SIZE = 64
TC = 16


def shifted(x, axis, by):
    peers = lax.axis_size(axis)
    pairs = [(i, i + by) for i in range(peers) if 0 <= i + by < peers]
    return lax.ppermute(x, axis, pairs)


def passed_along(x, axis, by):
    peers = lax.axis_size(axis)
    return lax.ppermute(x, axis, [(i, (i + by) % peers) for i in range(peers)])


def row_norm(values):
    return values * lax.rsqrt(jnp.mean(values * values, axis=-1, keepdims=True) + 1e-05)


def head_norm(values):
    return values * lax.rsqrt(jnp.mean(values * values, axis=-1, keepdims=True) + 1e-06)


def transposed_dot(a, b):
    return lax.dot_general(a, b, (((0,), (0,)), ((), ())), preferred_element_type=jnp.float32)


def rowwise_dot(a, b):
    return lax.dot_general(a, b, (((1,), (1,)), ((), ())), preferred_element_type=jnp.float32)


def plain_dot(a, b):
    return jnp.dot(a, b, preferred_element_type=jnp.float32)


def half_sums(x):
    low = lax.broadcasted_iota(jnp.int32, x.shape, 1) < HEAD_SIZE
    first = jnp.sum(jnp.where(low, x, 0.0), axis=1, keepdims=True)
    second = jnp.sum(jnp.where(low, 0.0, x), axis=1, keepdims=True)
    return jnp.where(low, first, second)


DIRECT_KEYS = 2
CHAINED = 2


def fits_planes(width):
    blocks, bands = lax.axis_size("blk"), lax.axis_size("grid")
    devices = blocks * bands
    return bands == 4 and blocks == 8 and width % devices == 0 and (width // devices) % 8 == 0


def chip_partner(bit, own_blk, own_grid):
    if bit == 0:
        mine = own_grid // 2
        return {"blk": own_blk, "grid": own_grid + (1 - 2 * mine) * 2}, mine
    step = 1 << (bit - 1)
    mine = own_blk // step % 2
    return {"blk": own_blk + (1 - 2 * mine) * step, "grid": own_grid}, mine


def layer_kernel(plan, *refs):
    nz, parts = plan
    (scale_hbm, tiles_hbm, grad_hbm, stem_hbm, gain_hbm, wqkv_hbm, wout_hbm, pos_hbm) = refs[:8]
    (stem_out, gain_out, qkv_out, out_out) = refs[8:12]
    scratch = list(refs[12:])
    count = len(parts)
    nb = len(parts[0][1])
    first = [scratch.pop(0) for _ in range(count)]
    recv = [[scratch.pop(0) for _ in range(nb - 1)] for _ in range(count)]
    send = [[None] + [scratch.pop(0) for _ in range(nb - 1)] for _ in range(count)]
    keep = [[scratch.pop(0) for _ in range(nb - 1)] for _ in range(count)]
    (final, final_keep, last_in, stem_w, wqkv, wout, image, halo_rows, grad_pair, hidden_pair, attn_pair, dq_pair, dkv_pair,
     kv, dkv_out, dkv_own, dkv_in, dkv_mid, dkv_side, normed_ref, inv_ref, qk_ref, heads_inv, qn, da, attn, dq, dqkv,
     tok_out, tok_all, stem_send, stem_got, stem_next, stem_last, gain_own, gain_got, gain_plane, gain_z, gain_col, gain_ref, pos_ref, scale_ref,
     load_sem, pair_send, pair_got, final_send, final_got, cross_got, halo_send, halo_got, tile_send, tile_got, pass_send, pass_got,
     kv_send, kv_got, dkv_send, dkv_got, part_send, part_got, tok_send, tok_got, gain_send, gain_arrived,
     gain_z_send, gain_z_got, stem_sent, stem_arrived) = scratch
    tok, width = grad_pair.shape[1:]
    halo = halo_rows.shape[0]
    pin = image.shape[2]
    span = kv.shape[0] * HEAD_SIZE
    group = QUERY_HEADS // KEY_VALUE_HEADS
    own_blk = lax.axis_index("blk")
    own_grid = lax.axis_index("grid")
    blk_count = lax.axis_size("blk")
    grid_count = lax.axis_size("grid")
    core = own_grid % 2
    own_y = own_grid // 2
    own_x = own_blk % 2
    own_z = own_blk // 2
    z_low, z_high = own_z % 2, own_z // 2
    rows = width // (blk_count * grid_count)
    other_core = {"blk": own_blk, "grid": own_grid + 1 - 2 * core}
    above = {"blk": own_blk, "grid": (own_grid + grid_count - 1) % grid_count}
    plane = [(i, j) for i in range(2) for j in range(grid_count) if i + j > 0]

    def along(offset):
        return {"blk": (own_blk + offset + blk_count) % blk_count, "grid": own_grid}

    def beside(i, j):
        return {"blk": own_z * 2 + (own_x + i) % 2, "grid": (own_grid + j) % grid_count}

    def level(k):
        return {"blk": (own_z + k) % nz * 2 + own_x, "grid": own_grid}

    z_near = {"blk": own_blk + (1 - 2 * z_low) * 2, "grid": own_grid}
    z_far = {"blk": own_blk + (1 - 2 * z_high) * 4, "grid": own_grid}

    own_rows = pl.ds(pl.multiple_of(own_grid * tok, tok), tok)
    loads = [
        pltpu.make_async_copy(tiles_hbm, image.at[own_x, own_rows], load_sem.at[0]),
        pltpu.make_async_copy(stem_hbm.at[0], stem_w.at[0], load_sem.at[1]),
        pltpu.make_async_copy(stem_hbm.at[1], stem_w.at[1], load_sem.at[2]),
        pltpu.make_async_copy(wqkv_hbm, wqkv, load_sem.at[3]),
        pltpu.make_async_copy(grad_hbm, grad_pair.at[core], load_sem.at[4]),
        pltpu.make_async_copy(wout_hbm, wout, load_sem.at[5]),
        pltpu.make_async_copy(gain_hbm, gain_ref, load_sem.at[6]),
        pltpu.make_async_copy(pos_hbm, pos_ref, load_sem.at[7]),
        pltpu.make_async_copy(scale_hbm, scale_ref, load_sem.at[8]),
    ]
    barrier = pltpu.get_barrier_semaphore()
    peers = [beside(i, j) for i, j in plane] + [level(k) for k in range(1, nz)] + [along(j) for j in (1, 2, 3, -1, -2, -3)]
    for peer in peers:
        pl.semaphore_signal(barrier, inc=1, device_id=peer, device_id_type=pl.DeviceIdType.MESH)
    for which in (0, 1, 2, 6, 3, 4, 5, 7, 8):
        loads[which].start()
    image[:, grid_count * tok :] = jnp.zeros((2, halo, pin), image.dtype)

    def push(source, target, sems, got, device):
        copy = pltpu.make_async_remote_copy(
            src_ref=source, dst_ref=target, send_sem=sems, recv_sem=got, device_id=device, device_id_type=pl.DeviceIdType.MESH
        )
        copy.start()
        return copy

    def all_of(ref, sems, got):
        return pltpu.make_async_remote_copy(
            src_ref=ref, dst_ref=ref, send_sem=sems, recv_sem=got, device_id=other_core, device_id_type=pl.DeviceIdType.MESH
        )

    def pair(which, source, target):
        return push(source, target, pair_send.at[which], pair_got.at[which], other_core)

    def tiles_to(slot, i, j):
        mine = image.at[own_x, own_rows]
        return push(mine, mine, tile_send.at[slot], tile_got.at[slot], beside(i, j))

    pl.semaphore_wait(barrier, len(peers))
    halo_copy = push(tiles_hbm.at[:halo], halo_rows, halo_send, halo_got, above)
    loads[0].wait()
    tile_copies = [tiles_to(0, 0, 2), tiles_to(1, 1, 0)]
    tile_pair = pair(0, image.at[own_x, own_rows], image.at[own_x, own_rows])

    loads[1].wait()
    tiles = image[own_x, own_rows]
    stem = plain_dot(tiles, stem_w[0])
    loads[2].wait()
    halo_copy.wait()

    @pl.when(own_grid == grid_count - 1)
    def _():
        halo_rows[...] = jnp.zeros(halo_rows.shape, halo_rows.dtype)

    below = jnp.concatenate([tiles[halo:], halo_rows[...]], axis=0)
    stem = stem + plain_dot(below, stem_w[1])
    token_f = stem.astype(jnp.bfloat16).astype(jnp.float32)
    inv = lax.rsqrt(jnp.sum(token_f * token_f, axis=1, keepdims=True) / width + 1e-05)
    normed = token_f * inv
    normed_ref[...] = normed
    inv_ref[...] = jnp.broadcast_to(inv, inv_ref.shape)
    loads[6].wait()
    gain_f = gain_ref[...].astype(jnp.float32).reshape(1, width)
    hidden = (normed * gain_f).astype(jnp.bfloat16)
    hidden_pair[core] = hidden
    loads[3].wait()
    key_start = QUERY_HEADS * HEAD_SIZE

    def normalize(x):
        scale = lax.rsqrt(half_sums(x * x) / HEAD_SIZE + 1e-06)
        return scale, (x * scale).astype(jnp.bfloat16)

    keys = plain_dot(hidden, wqkv[:, key_start:])
    def kv_push(g, source, slot, which, device):
        return push(kv.at[g, source], kv.at[g, slot], kv_send.at[which], kv_got.at[g, slot], device)

    def kv_copy(g, slot, which):
        return pltpu.make_async_remote_copy(
            src_ref=kv.at[g, 0], dst_ref=kv.at[g, slot], send_sem=kv_send.at[which], recv_sem=kv_got.at[g, slot],
            device_id=along(2), device_id_type=pl.DeviceIdType.MESH,
        )

    for u in range(span // 128):
        at = u * 128
        heads_inv[:, key_start + at : key_start + at + 128], key_n = normalize(keys[:, at : at + 128])
        value = keys[:, span + at : span + at + 128].astype(jnp.bfloat16)
        for e in range(2):
            g, lanes = 2 * u + e, slice(e * HEAD_SIZE, (e + 1) * HEAD_SIZE)
            kv[g, 0] = jnp.concatenate([key_n[:, lanes], value[:, lanes]], axis=1)
            kv_push(g, 0, 2, 0, along(2))
            if g < DIRECT_KEYS:
                kv_push(g, 0, 1 + 2 * own_x, 1, along(1 + 2 * own_x))
            else:

                @pl.when(own_x == 0)
                def _():
                    kv_push(g, 0, 1, 1, along(1))

    qk_ref[:, key_start:] = keys[:, :span]
    loads[4].wait()
    grad_copy = pair(1, grad_pair.at[core], grad_pair.at[core])
    hidden_copy = pair(2, hidden_pair.at[core], hidden_pair.at[core])
    queries = plain_dot(hidden, wqkv[:, :key_start])
    qk_ref[:, :key_start] = queries
    for at in range(0, key_start, 128):
        heads_inv[:, at : at + 128], qn[:, at : at + 128] = normalize(queries[:, at : at + 128])
    loads[5].wait()
    grad_own = grad_pair[core]
    da[...] = rowwise_dot(grad_own, wout[...]).astype(jnp.bfloat16)

    loads[7].wait()
    loads[8].wait()
    query_pos = pos_ref[pl.ds(own_blk, 1), :]
    seen = []
    for j in range(4):
        key_pos = pos_ref[pl.ds((own_blk + blk_count - j) % blk_count, 1), :]
        column = jnp.broadcast_to(key_pos, (tok, tok)).T
        seen.append(column <= query_pos)
    visible = jnp.concatenate([jnp.where(x, 1.0, 0.0) for x in seen], axis=0) > 0.5
    def pass_up(g):
        kv_copy(g, 1, 3).wait_recv()

        @pl.when(own_x == 0)
        def _():
            kv_push(g, 1, 3, 3, along(2))

    for g in range(KEY_VALUE_HEADS):
        kv_copy(g, 2, 0).wait_recv()
        kv_push(g, 2, 3 - 2 * own_x, 2, beside(1, 0))

    def dkv_push(source, g, slot, which, device):
        return push(source, dkv_in.at[g, slot], dkv_send.at[which], dkv_got.at[g, slot], device)

    def dkv_copy_of(g, slot, which):
        return pltpu.make_async_remote_copy(
            src_ref=dkv_out.at[g, 0], dst_ref=dkv_in.at[g, slot], send_sem=dkv_send.at[which], recv_sem=dkv_got.at[g, slot],
            device_id=along(2), device_id_type=pl.DeviceIdType.MESH,
        )

    def give(g):
        if g < CHAINED:
            dkv_push(dkv_out.at[g, 2 - 2 * own_x], g, 3 * own_x, 0, along(own_x - 2))
        else:
            dkv_push(dkv_out.at[g, 2 * own_x], g, 1, 1, beside(1, 0))
            dkv_push(dkv_out.at[g, 2 - 2 * own_x], g, 0, 0, along(2 * own_x - 3))

    def sideways(g):
        @pl.when(own_x == 0)
        def _():
            dkv_copy_of(g, 0, 0).wait_recv()
            dkv_side[g] = (dkv_out[g, 0].astype(jnp.float32) + dkv_in[g, 0].astype(jnp.float32)).astype(jnp.bfloat16)

        @pl.when(own_x == 1)
        def _():
            dkv_side[g] = dkv_out[g, 2]

        dkv_push(dkv_side.at[g], g, 1, 1, beside(1, 0))

    def combine(g):
        dkv_copy_of(g, 1, 1).wait_recv()
        dkv_mid[g] = (dkv_out[g, 1].astype(jnp.float32) + dkv_in[g, 1].astype(jnp.float32)).astype(jnp.bfloat16)
        dkv_push(dkv_mid.at[g], g, 2, 2, along(-2))

    for g in range(KEY_VALUE_HEADS):
        if g <= DIRECT_KEYS - 1 or g == KEY_VALUE_HEADS:
            kv_copy(g, 1, 3).wait_recv()
        kv_copy(g, 3, 2).wait_recv()
        if g == 2:
            tile_copies[1].wait()
            near = image.at[1 - own_x, own_rows]
            tile_copies.append(push(near, near, tile_send.at[2], tile_got.at[2], beside(0, 2)))
        keys_g = kv[g, :, :, :HEAD_SIZE].reshape(4 * tok, HEAD_SIZE)
        values_g = kv[g, :, :, HEAD_SIZE:].reshape(4 * tok, HEAD_SIZE)
        heads = [slice((g * group + i) * HEAD_SIZE, (g * group + i + 1) * HEAD_SIZE) for i in range(group)]
        queries_g = jnp.concatenate([qn[:, h] for h in heads], axis=0)
        grads_g = jnp.concatenate([da[:, h] for h in heads], axis=0)
        scores = rowwise_dot(keys_g, queries_g)
        dprobs = rowwise_dot(values_g, grads_g)
        probs, low = [], []
        for i in range(group):
            weights = jnp.where(visible, jnp.exp(scores[:, i * tok : (i + 1) * tok] * scale_ref[g * group + i]), 0.0)
            p = weights * (1.0 / jnp.sum(weights, axis=0, keepdims=True))
            probs.append(p)
            low.append(p.astype(jnp.bfloat16))
        low_g = jnp.concatenate(low, axis=1)
        attn_t = transposed_dot(values_g, low_g)
        delta = jnp.sum(grads_g.astype(jnp.float32).T * attn_t, axis=0, keepdims=True)
        ds = []
        for i in range(group):
            cols = slice(i * tok, (i + 1) * tok)
            ds.append((scale_ref[g * group + i] * probs[i] * (dprobs[:, cols] - delta[:, cols])).astype(jnp.bfloat16))
        ds_g = jnp.concatenate(ds, axis=1)
        dq_g = transposed_dot(keys_g, ds_g).T
        attn_g = attn_t.T
        for i in range(group):
            attn[:, heads[i]] = attn_g[i * tok : (i + 1) * tok].astype(jnp.bfloat16)
            dq[:, heads[i]] = dq_g[i * tok : (i + 1) * tok]
        dkeys = plain_dot(ds_g, queries_g).reshape(4, tok, HEAD_SIZE)
        dvalues = plain_dot(low_g, grads_g).reshape(4, tok, HEAD_SIZE)
        dkv_own[g] = jnp.concatenate([dkeys[0], dvalues[0]], axis=1)
        for j in (1, 2, 3):
            dkv_out[g, j - 1] = jnp.concatenate([dkeys[j], dvalues[j]], axis=1).astype(jnp.bfloat16)
        give(g)
        if g == 0:
            for h in range(DIRECT_KEYS, KEY_VALUE_HEADS):
                pass_up(h)
        if 0 <= g - 1 < CHAINED:
            sideways(g - 1)
    half = key_start // 2

    def half_of(start, amount, which):
        return pl.ds(pl.multiple_of(start + which * amount, 128), amount)

    attn_copy = pair(3, attn.at[:, half_of(0, half, 1 - core)], attn_pair.at[core])
    attn_pair[core] = attn[:, half_of(0, half, core)]

    def pull(at, g):
        scale = heads_inv[:, at : at + 128]
        x = qk_ref[:, at : at + 128] * scale
        return (scale * (g - x * (half_sums(g * x) / HEAD_SIZE))).astype(jnp.bfloat16)

    for at in range(0, key_start, 128):
        dqkv[:, at : at + 128] = pull(at, dq[:, at : at + 128])
    dq_copy = pair(4, dqkv.at[:, half_of(0, half, 1 - core)], dq_pair.at[core])
    dq_pair[core] = dqkv[:, half_of(0, half, core)]

    copies = [None] * count
    steps = [0] * count
    held_back = [2, 5]
    starts = [sum(w for _, _, w in parts[:p]) for p in range(count)]

    def transfer(p, source):
        partner = chip_partner(parts[p][1][steps[p]], own_blk, own_grid)[0]
        copies[p] = push(source, recv[p][steps[p]], part_send.at[steps[p]], part_got.at[p, steps[p]], partner)

    def begin(members, left, right):
        product = transposed_dot(left.reshape(2 * tok, width), right).astype(jnp.bfloat16)
        at = 0
        for p in members:
            order, w = parts[p][1:]
            first[p][...] = product[:, at : at + w].reshape(first[p].shape)
            at += w
            if p not in held_back:
                launch(p)

    def launch(p):
        mine = chip_partner(parts[p][1][0], own_blk, own_grid)[1]
        transfer(p, first[p].at[:, 1 - mine])

    def advance(p):
        step, order = steps[p], parts[p][1]
        copies[p].wait_recv()
        if step == nb - 1:
            cols = slice(starts[p], starts[p] + parts[p][2])
            final[:, cols] = keep[p][step - 1][core] + last_in[core, :, cols].astype(jnp.float32)
            return
        held = recv[p][step]
        mine = chip_partner(order[step], own_blk, own_grid)[1]
        left_over = [b for b in range(nb) if b not in order[:step]]
        inner = first[p].shape[2]

        def total(i):
            if step == 0:
                return first[p][i // inner, mine, i % inner].astype(jnp.float32) + held[i // inner, i % inner].astype(jnp.float32)
            return keep[p][step - 1][i] + held[i].astype(jnp.float32)

        steps[p] = step + 1
        left_over.remove(order[step])
        place_next = 1 << left_over.index(order[step + 1])
        mine_next = chip_partner(order[step + 1], own_blk, own_grid)[1]
        amount = 1 << (nb - 2 - step)
        if amount == 1:
            cols = slice(starts[p], starts[p] + parts[p][2])
            gone, kept = total(1 - mine_next), total(mine_next)
            partner = chip_partner(order[step + 1], own_blk, own_grid)[0]
            across = {"blk": partner["blk"], "grid": other_core["grid"]}
            for c in range(2):
                send[p][step + 1][c] = gone[c * rows : (c + 1) * rows].astype(jnp.bfloat16)
                keep[p][step][c] = kept[c * rows : (c + 1) * rows]
            target = last_in.at[core, :, cols]
            copies[p] = push(send[p][step + 1].at[core], target, part_send.at[step + 1], part_got.at[p, step + 1], partner)
            push(send[p][step + 1].at[1 - core], target, part_send.at[step + 1], cross_got, across)
            push(keep[p][step].at[1 - core], final_keep.at[:, cols], final_send, final_got, other_core)
            return
        for r in range(amount):
            away = r // place_next * (2 * place_next) + (1 - mine_next) * place_next + r % place_next
            send[p][step + 1][r] = total(away).astype(jnp.bfloat16)
        transfer(p, send[p][step + 1])
        for r in range(amount):
            here = r // place_next * (2 * place_next) + mine_next * place_next + r % place_next
            keep[p][step][r] = total(here)

    def advance_all(members):
        for p in members:
            advance(p)

    of_out, of_query, of_key = [[p for p in range(count) if parts[p][0] == m] for m in range(3)]
    combine(0)
    attn_copy.wait()
    grad_copy.wait()
    begin(of_out, grad_pair[...], attn_pair[...].reshape(2 * tok, half))
    for g in (2, 1, 3):
        combine(g)
    launch(of_out[2])
    dq_copy.wait()
    hidden_copy.wait()
    begin(of_query, hidden_pair[...], dq_pair[...].reshape(2 * tok, half))

    for slot, (i, j) in enumerate(((0, 2), (1, 0), (1, 2))):
        if slot != 1:
            tile_copies[slot].wait()
        where = image.at[(own_x + i) % 2, pl.ds(pl.multiple_of((own_grid + j) % grid_count * tok, tok), tok)]
        push(where, where, pass_send, pass_got, other_core)

    for g in range(KEY_VALUE_HEADS):
        if g < CHAINED:

            @pl.when(own_x == 0)
            def _():
                dkv_copy_of(g, 3, 0).wait_recv()
                dkv_own[g] += dkv_in[g, 3].astype(jnp.float32)

        else:
            dkv_copy_of(g, 0, 0).wait_recv()
        dkv_copy_of(g, 2, 2).wait_recv()
    for u in range(span // 128):
        sums = []
        for g in (2 * u, 2 * u + 1):
            total_kv = dkv_own[g] + dkv_in[g, 2].astype(jnp.float32)
            if g >= CHAINED:
                total_kv = total_kv + dkv_in[g, 0].astype(jnp.float32)
            sums.append(total_kv)
        at = key_start + u * 128
        dqkv[:, at : at + 128] = pull(at, jnp.concatenate([x[:, :HEAD_SIZE] for x in sums], axis=1))
        d_value = jnp.concatenate([x[:, HEAD_SIZE:] for x in sums], axis=1)
        dqkv[:, at + span : at + span + 128] = d_value.astype(jnp.bfloat16)
    dkv_copy = pair(5, dqkv.at[:, half_of(key_start, span, 1 - core)], dkv_pair.at[core])
    dkv_pair[core] = dqkv[:, half_of(key_start, span, core)]
    d_hidden = rowwise_dot(dqkv[...], wqkv[...])
    advance_all(of_out[:2])
    normed = normed_ref[...]
    flow = d_hidden * gain_f
    inner_mean = jnp.sum(flow * normed, axis=1, keepdims=True) / width
    d_tokens = grad_pair[core].astype(jnp.float32) + inv_ref[:, :1] * (flow - normed * inner_mean)
    turned = d_tokens.T
    for c in range(4 * 2):
        pieces = [turned[(r * 8 + c) * rows : (r * 8 + c + 1) * rows] for r in range(nz)]
        tok_out[c] = jnp.concatenate(pieces, axis=0).astype(jnp.bfloat16)
    own_lanes = pl.ds(pl.multiple_of(own_grid * tok, tok), tok)
    gain_own[...] = jnp.sum(d_hidden * normed, axis=0, keepdims=True)
    for i, j in plane:
        to_grid = (own_grid + j) % grid_count
        goal = (own_x + i) % 2 * grid_count + to_grid
        push(tok_out.at[goal], tok_all.at[own_x, :, own_lanes], tok_send, tok_got, beside(i, j))
    for slot, (i, j) in enumerate(plane):
        push(gain_own, gain_got.at[slot], gain_send, gain_arrived, beside(i, j))
    tok_all[own_x, :, own_lanes] = tok_out[own_x * grid_count + own_grid]

    launch(of_query[2])
    dkv_copy.wait()
    begin(of_key, hidden_pair[...], dkv_pair[...].reshape(2 * tok, span))
    advance_all(of_out[:2])
    advance(of_out[2])
    tile_pair.wait()
    all_of(image.at[0, : 3 * tok], pass_send, pass_got).wait()
    all_of(tok_out.at[: len(plane)], tok_send, tok_got).wait()
    chunks = stem_send.shape[0]
    step = pin // chunks
    stem_copies = []
    for h in range(chunks):
        cols = slice(h * step, (h + 1) * step)
        straight = plain_dot(tok_all[0], image[0, : grid_count * tok, cols]) + plain_dot(tok_all[1], image[1, : grid_count * tok, cols])
        lower = plain_dot(tok_all[0], image[0, halo:, cols]) + plain_dot(tok_all[1], image[1, halo:, cols])
        for r in range(nz):
            both = jnp.concatenate([straight[r * rows : (r + 1) * rows], lower[r * rows : (r + 1) * rows]], axis=0)
            stem_send[h, r % 2, r // 2] = both.astype(jnp.bfloat16)
        stem_copies.append(push(stem_send.at[h, 1 - z_low], stem_got.at[h], stem_sent.at[0], stem_arrived.at[h, 0], z_near))

    def stem_near(h, k):
        return stem_send[h, z_low, k].astype(jnp.float32) + stem_got[h, k].astype(jnp.float32)

    def stem_beyond(h):
        stem_copies[h].wait_recv()
        stem_next[h] = stem_near(h, 1 - z_high).astype(jnp.bfloat16)
        stem_copies[h] = push(stem_next.at[h], stem_last.at[h], stem_sent.at[1], stem_arrived.at[h, 1], z_far)

    all_of(gain_got, gain_send, gain_arrived).wait()
    gain_sum = gain_own[...]
    for slot in range(len(plane)):
        gain_sum = gain_sum + gain_got[slot]
    gain_plane[...] = gain_sum
    for k in range(1, nz):
        push(gain_plane, gain_z.at[k - 1], gain_z_send, gain_z_got, level(k))
    advance_all(of_query + of_out + of_key)
    for h in range(chunks):
        stem_beyond(h)
        if h == chunks // 2 - 1:
            advance_all(of_query)
    advance_all(of_key + of_out[2:])
    advance_all(of_query + of_out[:2] + of_key + of_out[2:])
    advance_all(of_query)
    all_of(gain_z, gain_z_send, gain_z_got).wait()
    gain_sum = gain_plane[...]
    for k in range(nz - 1):
        gain_sum = gain_sum + gain_z[k]
    gain_col[...] = jnp.broadcast_to(gain_sum, (128, width)).T
    own_gain = gain_col[pl.ds(pl.multiple_of((own_blk * grid_count + own_grid) * rows, 8), rows), :]
    square = jnp.concatenate([own_gain, jnp.zeros((128 - rows, 128), jnp.float32)], axis=0).T
    gain_out[...] = square[:1, :rows]
    advance_all(of_key)
    for h in range(chunks):
        stem_copies[h].wait_recv()
        total = stem_near(h, z_high) + stem_last[h].astype(jnp.float32)
        cols = slice(h * step, (h + 1) * step)
        stem_out[0, :, cols] = total[:rows]
        stem_out[1, :, cols] = total[rows:]
    all_of(final_keep, final_send, final_got).wait()
    all_of(last_in.at[0], final_send, cross_got).wait_recv()
    all_of(kv.at[:, 0], kv_send.at[0], final_got).wait_send()
    all_of(kv.at[:, 0], kv_send.at[2], final_got).wait_send()

    @pl.when(own_x == 0)
    def _():
        all_of(kv.at[:, 0], kv_send.at[1], final_got).wait_send()
        all_of(kv.at[DIRECT_KEYS:, 0], kv_send.at[3], final_got).wait_send()

    @pl.when(own_x == 1)
    def _():
        all_of(kv.at[:DIRECT_KEYS, 0], kv_send.at[1], final_got).wait_send()

    for which in range(3):
        all_of(dkv_mid, dkv_send.at[which], final_got).wait_send()
    for step in range(nb):
        amount = count * (1 << (nb - 1 - step)) * 2 * rows * 128 // pin
        all_of(image.at[0, :amount], part_send.at[step], final_got).wait_send()
    all_of(stem_got, stem_sent.at[0], final_got).wait_send()
    all_of(stem_last, stem_sent.at[1], final_got).wait_send()
    final_keep[...] += last_in[1 - core].astype(jnp.float32)
    for source, which in ((final, core), (final_keep, 1 - core)):
        out_out[:, half_of(0, half, which)] = source[:, :half]
        qkv_out[:, half_of(0, half, which)] = source[:, half : 2 * half]
        qkv_out[:, half_of(key_start, span, which)] = source[:, 2 * half :]


def unpack_kernel(*refs):
    half = len(refs) // 2
    for source, target in zip(refs[:half], refs[half:]):
        target[...] = source[...]


def whole_layer(tiles, grad_out, stem_weight, norm_gain, w_qkv, w_out, per_head_scale, positions):
    blk_count, grid_count = lax.axis_size("blk"), lax.axis_size("grid")
    nz = blk_count // 2
    tok, width = grad_out.shape
    pin = tiles.shape[1]
    qd, span = QUERY_HEADS * HEAD_SIZE, KEY_VALUE_HEADS * HEAD_SIZE
    rows = width // (blk_count * grid_count)
    rc = 2 * rows
    parts = []
    for m, orders in enumerate((((1, 0, 2, 3), (0, 1, 2, 3), (2, 1, 0, 3)), ((1, 0, 2, 3), (0, 1, 2, 3), (0, 1, 2, 3)), ((1, 0, 2, 3), (0, 1, 2, 3)))):
        parts += [(m, order, 128) for order in orders]
    nb = 4
    bf, f32 = jnp.bfloat16, jnp.float32
    firsts, recvs, sends, keeps = [], [], [], []
    for _, order, w in parts:
        inner = 1 << order[0]
        outer = (1 << nb) // (2 * inner)
        firsts.append(((outer, 2, inner, rc, w), bf))
        recvs.append(((outer, inner, rc, w), bf))
        for step in range(1, nb):
            shape = (1 << (nb - 1 - step), rc, w) if step < nb - 1 else (2, rows, w)
            if step < nb - 1:
                recvs.append((shape, bf))
            sends.append((shape, bf))
            keeps.append((shape, f32))
    total = sum(w for _, _, w in parts)
    chunks, heads = 4, KEY_VALUE_HEADS
    buffers = firsts + recvs + sends + keeps + [
        ((rows, total), f32),
        ((rows, total), f32),
        ((2, rows, total), bf),
        (stem_weight.shape, bf),
        (w_qkv.shape, bf),
        (w_out.shape, bf),
        ((2, grid_count * tok + TC, pin), bf),
        ((TC, pin), bf),
        ((2, tok, width), bf),
        ((2, tok, width), bf),
        ((2, tok, qd // 2), bf),
        ((2, tok, qd // 2), bf),
        ((2, tok, span), bf),
        ((heads, 4, tok, 2 * HEAD_SIZE), bf),
        ((heads, 3, tok, 2 * HEAD_SIZE), bf),
        ((heads, tok, 2 * HEAD_SIZE), f32),
        ((heads, 4, tok, 2 * HEAD_SIZE), bf),
        ((heads, tok, 2 * HEAD_SIZE), bf),
        ((heads, tok, 2 * HEAD_SIZE), bf),
        ((tok, width), f32),
        ((tok, 128), f32),
        ((tok, qd + span), f32),
        ((tok, qd + span), f32),
        ((tok, qd), bf),
        ((tok, qd), bf),
        ((tok, qd), bf),
        ((tok, qd), f32),
        ((tok, w_qkv.shape[1]), bf),
        ((2 * grid_count, nz * rows, tok), bf),
        ((2, nz * rows, grid_count * tok), bf),
        ((chunks, 2, nz // 2, rc, pin // chunks), bf),
        ((chunks, nz // 2, rc, pin // chunks), bf),
        ((chunks, rc, pin // chunks), bf),
        ((chunks, rc, pin // chunks), bf),
        ((1, width), f32),
        ((2 * grid_count - 1, 1, width), f32),
        ((1, width), f32),
        ((nz - 1, 1, width), f32),
        ((width, 128), f32),
        ((width,), bf),
        ((blk_count, tok), positions.dtype),
    ]
    dma = pltpu.SemaphoreType.DMA
    count = len(parts)
    semaphores = [dma((9,)), dma((6,)), dma((6,)), dma, dma, dma, dma, dma, dma((3,)), dma((3,)), dma, dma]
    semaphores += [dma((4,)), dma((heads, 4)), dma((3,)), dma((heads, 4)), dma((nb,)), dma((count, nb))]
    semaphores += [dma] * 6 + [dma((2,)), dma((chunks, 2))]
    vmem = pl.BlockSpec(memory_space=pltpu.VMEM)
    hbm = pl.BlockSpec(memory_space=pl.ANY)
    shapes = [
        jax.ShapeDtypeStruct(shape, f32)
        for shape in ((2, rows, pin), (1, rows), (rows, w_qkv.shape[1]), (rows, qd))
    ]
    inputs = (per_head_scale, tiles, grad_out, stem_weight, norm_gain, w_qkv, w_out, positions.reshape(-1, tok))
    results = pl.pallas_call(
        partial(layer_kernel, (nz, parts)),
        out_shape=shapes,
        in_specs=[hbm] * 8,
        out_specs=[vmem] * 4,
        scratch_shapes=[pltpu.VMEM(shape, kind) for shape, kind in buffers] + [pltpu.SMEM(per_head_scale.shape, f32)] + semaphores,
        compiler_params=pltpu.CompilerParams(collective_id=0, has_side_effects=True, vmem_limit_bytes=56000000),
    )(*[pltpu.with_memory_space_constraint(value, pltpu.HBM) for value in inputs])
    return pl.pallas_call(
        unpack_kernel,
        out_shape=shapes,
        in_specs=[vmem] * 4,
        out_specs=[vmem] * 4,
        compiler_params=pltpu.CompilerParams(vmem_limit_bytes=4000000),
    )(*results)


def shards(patches, stem_weight, norm_gain, w_qkv, w_out, per_head_scale, positions, d_out):
    tiles = patches[0]
    grad_out = d_out[0]
    if fits_planes(grad_out.shape[1]):
        d_stem, d_gain, d_qkv, d_out_t = whole_layer(
            tiles, grad_out, stem_weight, norm_gain, w_qkv, w_out, per_head_scale, positions
        )
        return (d_stem.transpose(0, 2, 1), d_gain.reshape(-1), d_qkv, d_out_t.T)
    token_rows = tiles.shape[0]
    group_factor = QUERY_HEADS // KEY_VALUE_HEADS
    query_span_width = QUERY_HEADS * HEAD_SIZE
    key_span_width = KEY_VALUE_HEADS * HEAD_SIZE
    arrived = shifted(tiles[:TC], "grid", -1)
    below = jnp.concatenate([tiles[TC:], arrived], axis=0)
    stem = jnp.dot(tiles, stem_weight[0], preferred_element_type=jnp.float32)
    stem = stem + jnp.dot(below, stem_weight[1], preferred_element_type=jnp.float32)
    token_f = lax.optimization_barrier(stem.astype(jnp.bfloat16)).astype(jnp.float32)
    gain_f = norm_gain.astype(jnp.float32)
    normed = row_norm(token_f)
    hidden = (normed * gain_f).astype(jnp.bfloat16)
    query_key_value = jnp.dot(hidden, w_qkv, preferred_element_type=jnp.float32)
    query = query_key_value[:, :query_span_width].reshape(token_rows, QUERY_HEADS, HEAD_SIZE)
    key = query_key_value[:, query_span_width : query_span_width + key_span_width].reshape(
        token_rows, KEY_VALUE_HEADS, HEAD_SIZE
    )
    query_normalized = head_norm(query).astype(jnp.bfloat16)
    key_n = head_norm(key).astype(jnp.bfloat16).reshape(token_rows, key_span_width)
    value = query_key_value[:, query_span_width + key_span_width :].astype(jnp.bfloat16)
    attention_gradient = jnp.dot(grad_out, w_out.T, preferred_element_type=jnp.float32).astype(
        jnp.bfloat16
    )
    kv_own = jnp.concatenate([key_n, value], axis=1)
    blk_count = lax.axis_size("blk")
    own_index = lax.axis_index("blk")
    blocks = [kv_own]
    for offset in range(1, 4):
        blocks.append(passed_along(kv_own, "blk", offset))
    causal_window = jnp.concatenate(blocks, axis=0)
    key_pos = jnp.concatenate(
        [
            lax.dynamic_slice_in_dim(
                positions, (own_index - offset) % blk_count * token_rows, token_rows
            )
            for offset in range(4)
        ]
    )
    query_pos = lax.dynamic_slice_in_dim(positions, own_index * token_rows, token_rows)
    visible = (key_pos[None, :] <= query_pos[:, None])[None]
    every_key = causal_window.shape[0]
    query_cube = query_normalized.reshape(token_rows, KEY_VALUE_HEADS, group_factor, HEAD_SIZE)
    gradient_cube = attention_gradient.reshape(token_rows, KEY_VALUE_HEADS, group_factor, HEAD_SIZE)
    key_cube = causal_window[:, :key_span_width].reshape(every_key, KEY_VALUE_HEADS, HEAD_SIZE)
    value_cube = causal_window[:, key_span_width:].reshape(every_key, KEY_VALUE_HEADS, HEAD_SIZE)
    score_scales = per_head_scale.reshape(KEY_VALUE_HEADS, group_factor)
    prob_list = []
    low_list = []
    attn_list = []
    for query_head_group in range(KEY_VALUE_HEADS):
        scale_col = score_scales[query_head_group][:, None, None]
        attention_scores = (
            jnp.einsum(
                "trd,sd->rts",
                query_cube[:, query_head_group],
                key_cube[:, query_head_group],
                preferred_element_type=jnp.float32,
            )
            * scale_col
        )
        attention_scores = jnp.where(visible, attention_scores, -1e30)
        top = jnp.max(attention_scores, axis=-1, keepdims=True)
        weights = jnp.where(visible, jnp.exp(attention_scores - top), 0.0)
        probs = weights / jnp.sum(weights, axis=-1, keepdims=True)
        probability_narrow = probs.astype(jnp.bfloat16)
        prob_list.append(probs)
        low_list.append(probability_narrow)
        attn_list.append(
            jnp.einsum(
                "rts,sd->trd",
                probability_narrow,
                value_cube[:, query_head_group],
                preferred_element_type=jnp.float32,
            )
        )
    attention_output = (
        jnp.stack(attn_list, axis=1).reshape(token_rows, query_span_width).astype(jnp.bfloat16)
    )
    dquery_list = []
    dkey_list = []
    dvalue_list = []
    for query_head_group in range(KEY_VALUE_HEADS):
        scale_col = score_scales[query_head_group][:, None, None]
        grad_group = gradient_cube[:, query_head_group]
        softmax_delta = jnp.sum(
            grad_group.astype(jnp.float32) * attn_list[query_head_group], axis=-1
        )
        probability_gradient = jnp.einsum(
            "trd,sd->rts",
            grad_group,
            value_cube[:, query_head_group],
            preferred_element_type=jnp.float32,
        )
        score_gradient = (
            scale_col
            * prob_list[query_head_group]
            * (probability_gradient - softmax_delta.T[:, :, None])
        ).astype(jnp.bfloat16)
        dquery_list.append(
            jnp.einsum(
                "rts,sd->trd",
                score_gradient,
                key_cube[:, query_head_group],
                preferred_element_type=jnp.float32,
            )
        )
        dkey_list.append(
            jnp.einsum(
                "rts,trd->sd",
                score_gradient,
                query_cube[:, query_head_group],
                preferred_element_type=jnp.float32,
            )
        )
        dvalue_list.append(
            jnp.einsum(
                "rts,trd->sd",
                low_list[query_head_group],
                grad_group,
                preferred_element_type=jnp.float32,
            )
        )
    query_gradient = jnp.stack(dquery_list, axis=1).reshape(token_rows, QUERY_HEADS, HEAD_SIZE)
    dkey_all = jnp.stack(dkey_list, axis=1).reshape(every_key, key_span_width)
    dvalue_all = jnp.stack(dvalue_list, axis=1).reshape(every_key, key_span_width)
    partial_terms = jnp.concatenate([dkey_all, dvalue_all], axis=1)
    pieces = [partial_terms[offset * token_rows : (offset + 1) * token_rows] for offset in range(4)]
    carried_state = pieces[0]
    for offset in (1, 2, 3):
        carried_state = carried_state + passed_along(pieces[offset], "blk", -offset)
    pull_query = jax.vjp(head_norm, query)[1]
    gather_key = jax.vjp(head_norm, key)[1]
    dq_full = pull_query(query_gradient)[0].reshape(token_rows, query_span_width)
    key_gradient_whole = gather_key(
        carried_state[:, :key_span_width].reshape(token_rows, KEY_VALUE_HEADS, HEAD_SIZE)
    )[0].reshape(token_rows, key_span_width)
    d_qkv = jnp.concatenate(
        [dq_full, key_gradient_whole, carried_state[:, key_span_width:]], axis=1
    ).astype(jnp.bfloat16)
    d_hidden = jnp.dot(d_qkv, w_qkv.T, preferred_element_type=jnp.float32)
    gain_term = jnp.sum(d_hidden * normed, axis=0)
    pull_tokens = jax.vjp(row_norm, token_f)[1]
    d_tokens = (grad_out.astype(jnp.float32) + pull_tokens(d_hidden * gain_f)[0]).astype(
        jnp.bfloat16
    )
    stem_term = jnp.stack(
        [
            jnp.dot(tiles.T, d_tokens, preferred_element_type=jnp.float32),
            jnp.dot(below.T, d_tokens, preferred_element_type=jnp.float32),
        ]
    )
    qkv_term = jnp.dot(hidden.T, d_qkv, preferred_element_type=jnp.float32)
    out_term = jnp.dot(attention_output.T, grad_out, preferred_element_type=jnp.float32)
    d_stem_weight = lax.psum_scatter(stem_term, ("blk", "grid"), scatter_dimension=2, tiled=True)
    d_norm_gain = lax.psum_scatter(gain_term, ("blk", "grid"), scatter_dimension=0, tiled=True)
    d_w_qkv = lax.psum_scatter(qkv_term, ("blk", "grid"), scatter_dimension=0, tiled=True)
    d_w_out = lax.psum_scatter(out_term, ("blk", "grid"), scatter_dimension=1, tiled=True)
    return (d_stem_weight, d_norm_gain, d_w_qkv, d_w_out)


def solution(mesh):
    placed = (P("grid", "blk", None), P(), P(), P(), P(), P(), P(), P("grid", "blk", None))
    return jax.shard_map(
        shards,
        mesh=mesh,
        in_specs=placed,
        out_specs=(
            P(None, None, ("blk", "grid")),
            P(("blk", "grid")),
            P(("blk", "grid"), None),
            P(None, ("blk", "grid")),
        ),
        check_vma=False,
    )
```
